768 devices in a mesh: ctx: 16 (over y_hi, x), sub: 48 (over z, y_lo, core).
Axes of the slice: x: 4, y: 8 (y_hi: 4, y_lo: 2; y = y_hi * 2 + y_lo), z: 12, core: 2. Of those that a mesh axis runs over, the one named last changes fastest.
Arguments:
- queries: bfloat16 [98304, 8, 128], P(('ctx', 'sub')), may hold values from -52 to 52
- key_rows: bfloat16 [98304, 128], P(('ctx', 'sub')), may hold values from -5 to 5
- value_rows: bfloat16 [98304, 128], P(('ctx', 'sub')), may hold values from -6 to 6
- block_docs: int32 [768], replicated, may hold values from 0 to 3, never falling along the last dimension, each value on 1 to 384 neighbouring positions
- windows: int32 [8], replicated, may hold values from 1 to 32, as said below
Outputs:
- attended: bfloat16 [98304, 8, 128], P(('ctx', 'sub'))
The draws below stay inside these ranges and needn't reach their ends.
Inputs may be any that keep to these rules, and one draw needn't show every extreme that they name: `windows`: some head's window is exactly 32 blocks.
All inputs are finite; a program needn't handle non-finite values.
Results may differ from the reference program's by a relative error of at most 0.0044.
Values may be sent and summed in bfloat16 or wider, within the bound.
A program may use at most 64 MiB of HBM per device.

```python
import math
import jax
import jax.numpy as jnp
import numpy as np
from jax import lax

H = 8
HD = 128
BLK = 128
WMAX = 32
TOKENS = 98304
NB = 768


def draw_pair(key):
    key_for_keys = jax.random.fold_in(key, 101)
    key_for_queries = jax.random.fold_in(key, 202)
    keys_drawn = jnp.clip(jax.random.normal(key_for_keys, (TOKENS, HD), jnp.float32), -5.0, 5.0)
    queries_drawn = jnp.clip(jax.random.normal(key_for_queries, (TOKENS, H, HD), jnp.float32), -5.0, 5.0)
    return (queries_drawn, keys_drawn)


def draw_queries(key, part):
    return draw_pair(key)[0].astype(jnp.bfloat16)


def draw_key_rows(key, part):
    return draw_pair(key)[1].astype(jnp.bfloat16)


def draw_windows(key, part):
    widths = jax.random.randint(jax.random.fold_in(key, 7), (H,), 1, WMAX)
    chosen = jax.random.randint(jax.random.fold_in(key, 9), (), 0, H)
    return jnp.where(jnp.arange(H, dtype=jnp.int32) == chosen, WMAX, widths).astype(jnp.int32)


def steps_of(key, dims, split, least, high):
    loudness, own = 1.0, jax.random.fold_in(key, 6)
    for dim, shards_of in split:
        draws = jnp.exp(jax.random.uniform(jax.random.fold_in(own, dim), (shards_of,), jnp.float32, least / len(split), high / len(split)))
        loudness = loudness * jnp.repeat(draws, dims[dim] // shards_of).reshape([-1 if axis == dim else 1 for axis in range(len(dims))])
    return loudness


def length_profile(amount, total, reach, lean):
    loads = [(1 << 20) // math.isqrt(rank ** lean) + 1 for rank in range(2, amount + 1)]
    spare, holding = total - reach - (amount - 1), [1] * (amount - 1)
    while spare > 0:
        candidates = [i for i in range(amount - 1) if holding[i] < reach]
        pool, left = sum([loads[i] for i in candidates]), spare
        for i in candidates:
            extra = min(reach - holding[i], max(1, left * loads[i] // pool), spare)
            holding[i] = holding[i] + extra
            spare = spare - extra
    return np.array([reach] + holding)


def ragged(own_key, amount, total, limit, skew):
    if amount == 2:
        one = jax.random.randint(own_key, (), max(1, total - limit), min(limit, total - 1) + 1)
        return jnp.stack([one, total - one])
    lengths = jnp.asarray(length_profile(amount, total, limit, skew), jnp.int32)
    couples = (amount - 1) // 2
    source_of, taker = lengths[1:1 + 2 * couples:2], lengths[2:2 + 2 * couples:2]
    margin = jnp.minimum(source_of - 1, limit - taker)
    passed = jax.random.randint(jax.random.fold_in(own_key, 1), (couples,), 0, 1 << 20) % (margin + 1)
    lengths = lengths.at[1:1 + 2 * couples:2].set(source_of - passed).at[2:2 + 2 * couples:2].set(taker + passed)
    return lengths[jax.random.permutation(jax.random.fold_in(own_key, 2), amount)]


def gaussian(stream_key, shape, width, limit, split=(), kind=jnp.bfloat16):
    loudness = steps_of(stream_key, shape, split, -0.22, 0.18) if split else 1.0
    drawn = jax.random.normal(stream_key, shape, jnp.float32) * width * loudness
    return jnp.minimum(jnp.maximum(drawn, -limit), limit).astype(kind)


def setup_inputs(seed: int = 0) -> dict:
    seeds = jax.random.split(jax.random.key(seed), 6)
    queries = draw_queries(jax.random.fold_in(seeds[5], 71), 0)
    key_rows = draw_key_rows(jax.random.fold_in(seeds[5], 71), 0)
    value_rows = gaussian(seeds[2], (TOKENS, HD), 1.0, 6.0, ((0, 768),))
    block_docs = jnp.searchsorted(jnp.cumsum(ragged(seeds[3], 4, NB, NB // 2, 1)), jnp.arange(NB), side="right").astype(jnp.int32)
    windows = draw_windows(jax.random.fold_in(seeds[5], 71), 0)
    return {"queries": queries, "key_rows": key_rows, "value_rows": value_rows, "block_docs": block_docs, "windows": windows}


def reference(queries, key_rows, value_rows, block_docs, windows):
    key_span = WMAX * BLK
    factor = HD ** -0.5

    def one_block(query_block):
        first_row = query_block * BLK
        key_first = jnp.maximum(first_row + BLK - key_span, 0).astype(jnp.int32)
        query_part = lax.dynamic_slice_in_dim(queries, first_row, BLK, 0).astype(jnp.float32)
        key_part = lax.dynamic_slice_in_dim(key_rows, key_first, key_span, 0).astype(jnp.float32)
        value_part = lax.dynamic_slice_in_dim(value_rows, key_first, key_span, 0).astype(jnp.float32)
        query_places = first_row + jnp.arange(BLK, dtype=jnp.int32)
        key_places = key_first + jnp.arange(key_span, dtype=jnp.int32)
        key_blocks = key_places // BLK
        same_doc = block_docs[key_blocks] == block_docs[query_block]
        causal = key_places[None, :] <= query_places[:, None]
        in_window = (query_block - key_blocks)[None, :] < windows[:, None]
        allowed = (same_doc[None, :] & causal)[:, None, :] & in_window[None, :, :]
        logits = jnp.einsum("qhd,kd->qhk", query_part, key_part) * factor
        masked = jnp.where(allowed, logits, -jnp.inf)
        highest = jnp.max(masked, axis=2)
        weights = jnp.where(allowed, jnp.exp(masked - highest[:, :, None]), 0.0).astype(jnp.bfloat16)
        denominator = jnp.sum(weights.astype(jnp.float32), axis=2)
        numerator = jnp.einsum("qhk,kd->qhd", weights.astype(jnp.float32), value_part)
        return (numerator / denominator[:, :, None]).astype(jnp.bfloat16)

    result = lax.map(one_block, jnp.arange(NB, dtype=jnp.int32))
    return result.reshape(TOKENS, H, HD)
```

```python
import functools

import jax
import jax.numpy as jnp
from jax import lax
from jax.experimental import pallas as pl
from jax.experimental.pallas import tpu as pltpu
from jax.sharding import PartitionSpec as P

BLK = 128
WMAX = 32
LEVEL = 4
DEPTH = (WMAX - 1 + LEVEL - 1) // LEVEL + 1
MESH = pl.DeviceIdType.MESH


def relay_kernel(n_ctx, n_sub, kv_ref, got_ref, recv_sem, relay_sem, sib_sem, cross_sem, fwd_sem, own_sem):
    c = lax.axis_index("ctx")
    s = lax.axis_index("sub")
    total = n_ctx * n_sub
    g = c * n_sub + s
    q = s % LEVEL
    succ_g = (g + LEVEL) % total
    pred_g = (g + total - LEVEL) % total
    succ = (succ_g // n_sub, succ_g % n_sub)
    pred = (pred_g // n_sub, pred_g % n_sub)
    sib_q = q + 1 - 2 * (q % 2)
    cross_q = q + 2 - 4 * ((q // 2) % 2)
    sib = (c, s - q + sib_q)
    cross = (c, s - q + cross_q)

    barrier = pltpu.get_barrier_semaphore()
    for peer in (succ, pred, sib, cross):
        pl.semaphore_signal(barrier, inc=1, device_id=peer, device_id_type=MESH)
    pl.semaphore_wait(barrier, 4)

    own = pltpu.make_async_copy(kv_ref, got_ref.at[0, q], own_sem.at[0])
    own.start()

    def remote(src, k, col, peer, sem):
        return pltpu.make_async_remote_copy(
            src_ref=src,
            dst_ref=got_ref.at[k, col],
            send_sem=sem,
            recv_sem=recv_sem.at[k, col],
            device_id=peer,
            device_id_type=MESH,
        )

    sends = []
    for k in range(DEPTH):
        src = kv_ref if k == 0 else got_ref.at[k, q]
        if k > 0:
            remote(src, k, q, pred, relay_sem.at[k - 1]).wait_recv()
        if k + 1 < DEPTH:
            cp = remote(src, k + 1, q, succ, relay_sem.at[k])
            cp.start()
            sends.append(cp)
        cp = remote(src, k, q, sib, sib_sem.at[k])
        cp.start()
        sends.append(cp)
        cp = remote(src, k, q, cross, cross_sem.at[k])
        cp.start()
        sends.append(cp)
        got_cross = got_ref.at[k, cross_q]
        remote(got_cross, k, cross_q, cross, cross_sem.at[k]).wait_recv()
        cp = remote(got_cross, k, cross_q, sib, fwd_sem.at[k])
        cp.start()
        sends.append(cp)

    far_q = 3 - q
    for k in range(DEPTH):
        remote(got_ref.at[k, sib_q], k, sib_q, sib, sib_sem.at[k]).wait_recv()
        remote(got_ref.at[k, far_q], k, far_q, sib, fwd_sem.at[k]).wait_recv()
    for cp in sends:
        cp.wait_send()
    own.wait()


def relay(kv, n_ctx, n_sub):
    return pl.pallas_call(
        functools.partial(relay_kernel, n_ctx, n_sub),
        out_shape=jax.ShapeDtypeStruct((DEPTH, LEVEL) + kv.shape, kv.dtype),
        in_specs=[pl.BlockSpec(memory_space=pltpu.VMEM)],
        out_specs=pl.BlockSpec(memory_space=pl.ANY),
        scratch_shapes=[
            pltpu.SemaphoreType.DMA((DEPTH, LEVEL)),
            pltpu.SemaphoreType.DMA((DEPTH,)),
            pltpu.SemaphoreType.DMA((DEPTH,)),
            pltpu.SemaphoreType.DMA((DEPTH,)),
            pltpu.SemaphoreType.DMA((DEPTH,)),
            pltpu.SemaphoreType.DMA((1,)),
        ],
        compiler_params=pltpu.CompilerParams(collective_id=0, has_side_effects=True),
    )(kv)


def attend_kernel(ok_ref, dist_ref, q_ref, got_ref, win_ref, out_ref, s_sc, m_sc, num_sc, den_sc):
    rows, hd = q_ref.shape
    chunk = s_sc.shape[1]
    slots = s_sc.shape[0]
    heads = rows // BLK
    scale = hd ** -0.5

    def one_chunk(ci, carry):
        r0 = pl.multiple_of(ci * chunk, chunk)
        qc = q_ref[pl.ds(r0, chunk), :]
        win = win_ref[pl.ds(r0, chunk), :]
        query_i = (lax.broadcasted_iota(jnp.int32, (chunk, BLK), 0) + r0) // heads
        key_j = lax.broadcasted_iota(jnp.int32, (chunk, BLK), 1)
        m_sc[...] = jnp.full(m_sc.shape, -jnp.inf, jnp.float32)
        num_sc[...] = jnp.zeros(num_sc.shape, jnp.float32)
        den_sc[...] = jnp.zeros(den_sc.shape, jnp.float32)

        def first(slot, c2):
            d = dist_ref[slot]

            @pl.when(ok_ref[slot] != 0)
            def _():
                kb = got_ref[slot // LEVEL, slot % LEVEL, 0]
                sc = lax.dot_general(qc, kb, (((1,), (1,)), ((), ())), preferred_element_type=jnp.float32) * scale
                allowed = (d < win) & ((d > 0) | (key_j <= query_i))
                sc = jnp.where(allowed, sc, -jnp.inf)
                s_sc[slot] = sc
                m_sc[...] = jnp.maximum(m_sc[...], jnp.max(sc, axis=1, keepdims=True))

            return c2

        lax.fori_loop(0, slots, first, 0)

        def second(slot, c2):
            @pl.when(ok_ref[slot] != 0)
            def _():
                w = jnp.exp(s_sc[slot] - m_sc[...]).astype(jnp.bfloat16)
                vb = got_ref[slot // LEVEL, slot % LEVEL, 1]
                num_sc[...] += jnp.dot(w, vb, preferred_element_type=jnp.float32)
                den_sc[...] += jnp.sum(w.astype(jnp.float32), axis=1, keepdims=True)

            return c2

        lax.fori_loop(0, slots, second, 0)
        out_ref[pl.ds(r0, chunk), :] = (num_sc[...] / den_sc[...]).astype(out_ref.dtype)
        return carry

    lax.fori_loop(0, rows // chunk, one_chunk, 0)


def attend(ok, dist, q2, got, win_rows):
    rows, hd = q2.shape
    chunk = 256
    slots = DEPTH * LEVEL
    return pl.pallas_call(
        attend_kernel,
        out_shape=jax.ShapeDtypeStruct((rows, hd), q2.dtype),
        in_specs=[
            pl.BlockSpec(memory_space=pltpu.SMEM),
            pl.BlockSpec(memory_space=pltpu.SMEM),
            pl.BlockSpec(memory_space=pltpu.VMEM),
            pl.BlockSpec(memory_space=pltpu.VMEM),
            pl.BlockSpec(memory_space=pltpu.VMEM),
        ],
        out_specs=pl.BlockSpec(memory_space=pltpu.VMEM),
        scratch_shapes=[
            pltpu.VMEM((slots, chunk, BLK), jnp.float32),
            pltpu.VMEM((chunk, 1), jnp.float32),
            pltpu.VMEM((chunk, hd), jnp.float32),
            pltpu.VMEM((chunk, 1), jnp.float32),
        ],
        compiler_params=pltpu.CompilerParams(vmem_limit_bytes=48 * 1024 * 1024),
    )(ok, dist, q2, got, win_rows)


def local(queries, key_rows, value_rows, block_docs, windows):
    n_ctx = lax.axis_size("ctx")
    n_sub = lax.axis_size("sub")
    c = lax.axis_index("ctx")
    s = lax.axis_index("sub")
    g = c * n_sub + s
    q = s % LEVEL
    rows_here, heads, hd = queries.shape
    kv = jnp.stack([key_rows, value_rows])
    got = relay(kv, n_ctx, n_sub)

    k_of = jnp.arange(DEPTH * LEVEL, dtype=jnp.int32) // LEVEL
    col_of = jnp.arange(DEPTH * LEVEL, dtype=jnp.int32) % LEVEL
    dist = LEVEL * k_of + q - col_of
    key_block = g - dist
    doc_here = block_docs[g]
    doc_there = jnp.take(block_docs, jnp.clip(key_block, 0, block_docs.shape[0] - 1))
    ok = (dist >= 0) & (dist < WMAX) & (key_block >= 0) & (doc_there == doc_here)
    win_rows = jnp.tile(windows, rows_here).reshape(rows_here * heads, 1)
    out = attend(ok.astype(jnp.int32), dist, queries.reshape(rows_here * heads, hd), got, win_rows)
    return out.reshape(rows_here, heads, hd)


def solution(mesh):
    in_specs = (
        P(("ctx", "sub"), None, None),
        P(("ctx", "sub"), None),
        P(("ctx", "sub"), None),
        P(),
        P(),
    )
    out_specs = P(("ctx", "sub"), None, None)
    return jax.shard_map(local, mesh=mesh, in_specs=in_specs, out_specs=out_specs, check_vma=False)
```

```python
import functools

import jax
import jax.numpy as jnp
from jax import lax
from jax.experimental import pallas as pl
from jax.experimental.pallas import tpu as pltpu
from jax.sharding import PartitionSpec as P

BLK = 128
WMAX = 32
LEVEL = 4
DEPTH = (WMAX - 1 + LEVEL - 1) // LEVEL + 1
MESH = pl.DeviceIdType.MESH


def relay_kernel(n_ctx, n_sub, kv_ref, got_ref, recv_sem, relay_sem, sib_sem, cross_sem, fwd_sem, own_sem):
    c = lax.axis_index("ctx")
    s = lax.axis_index("sub")
    total = n_ctx * n_sub
    g = c * n_sub + s
    q = s % LEVEL
    succ_g = (g + LEVEL) % total
    pred_g = (g + total - LEVEL) % total
    succ = (succ_g // n_sub, succ_g % n_sub)
    pred = (pred_g // n_sub, pred_g % n_sub)
    sib_q = q + 1 - 2 * (q % 2)
    cross_q = q + 2 - 4 * ((q // 2) % 2)
    sib = (c, s - q + sib_q)
    cross = (c, s - q + cross_q)

    barrier = pltpu.get_barrier_semaphore()
    for peer in (succ, pred, sib, cross):
        pl.semaphore_signal(barrier, inc=1, device_id=peer, device_id_type=MESH)
    pl.semaphore_wait(barrier, 4)

    own = pltpu.make_async_copy(kv_ref, got_ref.at[0, q], own_sem.at[0])
    own.start()

    def remote(src, k, col, peer, sem):
        return pltpu.make_async_remote_copy(
            src_ref=src,
            dst_ref=got_ref.at[k, col],
            send_sem=sem,
            recv_sem=recv_sem.at[k, col],
            device_id=peer,
            device_id_type=MESH,
        )

    sends = []
    for k in range(DEPTH):
        src = kv_ref if k == 0 else got_ref.at[k, q]
        if k > 0:
            remote(src, k, q, pred, relay_sem.at[k - 1]).wait_recv()
        if k + 1 < DEPTH:
            cp = remote(src, k + 1, q, succ, relay_sem.at[k])
            cp.start()
            sends.append(cp)
        cp = remote(src, k, q, cross, cross_sem.at[k])
        cp.start()
        sends.append(cp)
        cp = remote(src, k, q, sib, sib_sem.at[k])
        cp.start()
        sends.append(cp)

    for k in range(DEPTH):
        got_cross = got_ref.at[k, cross_q]
        remote(got_cross, k, cross_q, cross, cross_sem.at[k]).wait_recv()
        cp = remote(got_cross, k, cross_q, sib, fwd_sem.at[k])
        cp.start()
        sends.append(cp)

    far_q = 3 - q
    for k in range(DEPTH):
        remote(got_ref.at[k, sib_q], k, sib_q, sib, sib_sem.at[k]).wait_recv()
        remote(got_ref.at[k, far_q], k, far_q, sib, fwd_sem.at[k]).wait_recv()
    for cp in sends:
        cp.wait_send()
    own.wait()


def relay(kv, n_ctx, n_sub):
    return pl.pallas_call(
        functools.partial(relay_kernel, n_ctx, n_sub),
        out_shape=jax.ShapeDtypeStruct((DEPTH, LEVEL) + kv.shape, kv.dtype),
        in_specs=[pl.BlockSpec(memory_space=pltpu.VMEM)],
        out_specs=pl.BlockSpec(memory_space=pl.ANY),
        scratch_shapes=[
            pltpu.SemaphoreType.DMA((DEPTH, LEVEL)),
            pltpu.SemaphoreType.DMA((DEPTH,)),
            pltpu.SemaphoreType.DMA((DEPTH,)),
            pltpu.SemaphoreType.DMA((DEPTH,)),
            pltpu.SemaphoreType.DMA((DEPTH,)),
            pltpu.SemaphoreType.DMA((1,)),
        ],
        compiler_params=pltpu.CompilerParams(collective_id=0, has_side_effects=True),
    )(kv)


def attend_kernel(ok_ref, dist_ref, q_ref, got_ref, win_ref, out_ref, s_sc, m_sc, num_sc, den_sc):
    rows, hd = q_ref.shape
    chunk = s_sc.shape[1]
    slots = s_sc.shape[0]
    heads = rows // BLK
    scale = hd ** -0.5

    def one_chunk(ci, carry):
        r0 = pl.multiple_of(ci * chunk, chunk)
        qc = q_ref[pl.ds(r0, chunk), :]
        query_i = (lax.broadcasted_iota(jnp.int32, (chunk, BLK), 0) + r0) // heads
        key_j = lax.broadcasted_iota(jnp.int32, (chunk, BLK), 1)
        causal = key_j <= query_i
        m_sc[...] = jnp.full(m_sc.shape, -jnp.inf, jnp.float32)
        num_sc[...] = jnp.zeros(num_sc.shape, jnp.float32)
        den_sc[...] = jnp.zeros(den_sc.shape, jnp.float32)

        def first(slot, c2):
            d = dist_ref[slot]

            @pl.when(ok_ref[slot] != 0)
            def _():
                kb = got_ref[slot // LEVEL, slot % LEVEL, 0]
                sc = lax.dot_general(qc, kb, (((1,), (1,)), ((), ())), preferred_element_type=jnp.float32) * scale
                allowed = (win_ref[pl.ds(r0, chunk), :] > d) & (causal | (d > 0))
                sc = jnp.where(allowed, sc, -jnp.inf)
                s_sc[slot] = sc
                m_sc[...] = jnp.maximum(m_sc[...], sc)

            return c2

        lax.fori_loop(0, slots, first, 0)
        m = jnp.max(m_sc[...], axis=1, keepdims=True)

        def second(slot, c2):
            @pl.when(ok_ref[slot] != 0)
            def _():
                w = jnp.exp(s_sc[slot] - m).astype(jnp.bfloat16)
                vb = got_ref[slot // LEVEL, slot % LEVEL, 1]
                num_sc[...] += jnp.dot(w, vb, preferred_element_type=jnp.float32)
                den_sc[...] += w.astype(jnp.float32)

            return c2

        lax.fori_loop(0, slots, second, 0)
        den = jnp.sum(den_sc[...], axis=1, keepdims=True)
        out_ref[pl.ds(r0, chunk), :] = (num_sc[...] / den).astype(out_ref.dtype)
        return carry

    lax.fori_loop(0, rows // chunk, one_chunk, 0)


def attend(ok, dist, q2, got, win_rows):
    rows, hd = q2.shape
    chunk = 512
    slots = DEPTH * LEVEL
    return pl.pallas_call(
        attend_kernel,
        out_shape=jax.ShapeDtypeStruct((rows, hd), q2.dtype),
        in_specs=[
            pl.BlockSpec(memory_space=pltpu.SMEM),
            pl.BlockSpec(memory_space=pltpu.SMEM),
            pl.BlockSpec(memory_space=pltpu.VMEM),
            pl.BlockSpec(memory_space=pltpu.VMEM),
            pl.BlockSpec(memory_space=pltpu.VMEM),
        ],
        out_specs=pl.BlockSpec(memory_space=pltpu.VMEM),
        scratch_shapes=[
            pltpu.VMEM((slots, chunk, BLK), jnp.float32),
            pltpu.VMEM((chunk, BLK), jnp.float32),
            pltpu.VMEM((chunk, hd), jnp.float32),
            pltpu.VMEM((chunk, BLK), jnp.float32),
        ],
        compiler_params=pltpu.CompilerParams(vmem_limit_bytes=48 * 1024 * 1024),
    )(ok, dist, q2, got, win_rows)


def local(queries, key_rows, value_rows, block_docs, windows):
    n_ctx = lax.axis_size("ctx")
    n_sub = lax.axis_size("sub")
    c = lax.axis_index("ctx")
    s = lax.axis_index("sub")
    g = c * n_sub + s
    q = s % LEVEL
    rows_here, heads, hd = queries.shape
    kv = jnp.stack([key_rows, value_rows])
    got = relay(kv, n_ctx, n_sub)

    k_of = jnp.arange(DEPTH * LEVEL, dtype=jnp.int32) // LEVEL
    col_of = jnp.arange(DEPTH * LEVEL, dtype=jnp.int32) % LEVEL
    dist = LEVEL * k_of + q - col_of
    key_block = g - dist
    doc_here = block_docs[g]
    doc_there = jnp.take(block_docs, jnp.clip(key_block, 0, block_docs.shape[0] - 1))
    ok = (dist >= 0) & (dist < WMAX) & (key_block >= 0) & (doc_there == doc_here)
    win_rows = jnp.broadcast_to(jnp.tile(windows, rows_here)[:, None], (rows_here * heads, BLK))
    out = attend(ok.astype(jnp.int32), dist, queries.reshape(rows_here * heads, hd), got, win_rows)
    return out.reshape(rows_here, heads, hd)


def solution(mesh):
    in_specs = (
        P(("ctx", "sub"), None, None),
        P(("ctx", "sub"), None),
        P(("ctx", "sub"), None),
        P(),
        P(),
    )
    out_specs = P(("ctx", "sub"), None, None)
    return jax.shard_map(local, mesh=mesh, in_specs=in_specs, out_specs=out_specs, check_vma=False)
```

```python
import functools

import jax
import jax.numpy as jnp
from jax import lax
from jax.experimental import pallas as pl
from jax.experimental.pallas import tpu as pltpu
from jax.sharding import PartitionSpec as P

BLK = 128
WMAX = 32
LEVEL = 4
DEPTH = (WMAX - 1 + LEVEL - 1) // LEVEL + 1
MESH = pl.DeviceIdType.MESH
CHUNK = 256


def fused_kernel(n_ctx, n_sub, ok_ref, kv_ref, q_ref, win_ref, out_ref,
                 got, s_sc, m_sc, num_sc, den_sc,
                 recv_sem, relay_sem, sib_sem, cross_sem, fwd_sem, own_sem):
    c = lax.axis_index("ctx")
    s = lax.axis_index("sub")
    total = n_ctx * n_sub
    g = c * n_sub + s
    q = s % LEVEL
    succ_g = (g + LEVEL) % total
    pred_g = (g + total - LEVEL) % total
    succ = (succ_g // n_sub, succ_g % n_sub)
    pred = (pred_g // n_sub, pred_g % n_sub)
    sib_q = q + 1 - 2 * (q % 2)
    cross_q = q + 2 - 4 * ((q // 2) % 2)
    far_q = 3 - q
    sib = (c, s - q + sib_q)
    cross = (c, s - q + cross_q)
    rows, hd = q_ref.shape
    heads = rows // BLK
    scale = hd ** -0.5
    n_chunks = rows // CHUNK

    barrier = pltpu.get_barrier_semaphore()
    for peer in (succ, pred, sib, cross):
        pl.semaphore_signal(barrier, inc=1, device_id=peer, device_id_type=MESH)
    pl.semaphore_wait(barrier, 4)

    own = pltpu.make_async_copy(kv_ref, got.at[0, q], own_sem.at[0])
    own.start()

    def remote(src, k, col, peer, sem):
        return pltpu.make_async_remote_copy(
            src_ref=src,
            dst_ref=got.at[k, col],
            send_sem=sem,
            recv_sem=recv_sem.at[k, col],
            device_id=peer,
            device_id_type=MESH,
        )

    m_sc[...] = jnp.full(m_sc.shape, -jnp.inf, jnp.float32)

    def logits(k, col):
        slot = k * LEVEL + col
        d = LEVEL * k + q - col
        live = ok_ref[slot] != 0

        def body(ci, carry):
            r0 = pl.multiple_of(ci * CHUNK, CHUNK)
            qc = q_ref[pl.ds(r0, CHUNK), :]
            kb = got[k, col, 0]
            sc = lax.dot_general(qc, kb, (((1,), (1,)), ((), ())), preferred_element_type=jnp.float32) * scale
            query_i = (lax.broadcasted_iota(jnp.int32, (CHUNK, BLK), 0) + r0) // heads
            key_j = lax.broadcasted_iota(jnp.int32, (CHUNK, BLK), 1)
            allowed = (win_ref[pl.ds(r0, CHUNK), :] > d) & ((key_j <= query_i) | (d > 0)) & live
            sc = jnp.where(allowed, sc, -jnp.inf)
            s_sc[slot, pl.ds(r0, CHUNK), :] = sc
            m_sc[pl.ds(r0, CHUNK), :] = jnp.maximum(m_sc[pl.ds(r0, CHUNK), :], sc)
            return carry

        lax.fori_loop(0, n_chunks, body, 0)

    remote(kv_ref, 1, q, succ, relay_sem.at[0]).start()
    remote(kv_ref, 0, q, cross, cross_sem.at[0]).start()
    remote(kv_ref, 0, q, sib, sib_sem.at[0]).start()
    own.wait()
    logits(0, q)

    def relay_step(k, carry):
        src = got.at[k, q]
        remote(src, k, q, pred, relay_sem.at[k - 1]).wait_recv()

        @pl.when(k + 1 < DEPTH)
        def _():
            remote(src, k + 1, q, succ, relay_sem.at[k]).start()

        remote(src, k, q, cross, cross_sem.at[k]).start()
        remote(src, k, q, sib, sib_sem.at[k]).start()
        logits(k, q)
        return carry

    lax.fori_loop(1, DEPTH, relay_step, 0)

    def cross_step(k, carry):
        src = got.at[k, cross_q]
        remote(src, k, cross_q, cross, cross_sem.at[k]).wait_recv()
        remote(src, k, cross_q, sib, fwd_sem.at[k]).start()
        logits(k, cross_q)
        return carry

    lax.fori_loop(0, DEPTH, cross_step, 0)

    def sib_step(k, carry):
        remote(got.at[k, sib_q], k, sib_q, sib, sib_sem.at[k]).wait_recv()
        logits(k, sib_q)
        remote(got.at[k, far_q], k, far_q, sib, fwd_sem.at[k]).wait_recv()
        logits(k, far_q)
        return carry

    lax.fori_loop(0, DEPTH, sib_step, 0)

    num_sc[...] = jnp.zeros(num_sc.shape, jnp.float32)
    den_sc[...] = jnp.zeros(den_sc.shape, jnp.float32)

    def weigh_chunk(ci, carry):
        r0 = pl.multiple_of(ci * CHUNK, CHUNK)
        m = jnp.max(m_sc[pl.ds(r0, CHUNK), :], axis=1, keepdims=True)

        def weigh(slot, c2):
            w = jnp.exp(s_sc[slot, pl.ds(r0, CHUNK), :] - m).astype(jnp.bfloat16)
            vb = got[slot // LEVEL, slot % LEVEL, 1]
            num_sc[pl.ds(r0, CHUNK), :] += jnp.dot(w, vb, preferred_element_type=jnp.float32)
            den_sc[pl.ds(r0, CHUNK), :] += w.astype(jnp.float32)
            return c2

        lax.fori_loop(0, DEPTH * LEVEL, weigh, 0)
        den = jnp.sum(den_sc[pl.ds(r0, CHUNK), :], axis=1, keepdims=True)
        out_ref[pl.ds(r0, CHUNK), :] = (num_sc[pl.ds(r0, CHUNK), :] / den).astype(out_ref.dtype)
        return carry

    lax.fori_loop(0, n_chunks, weigh_chunk, 0)

    def drain(k, carry):
        @pl.when(k + 1 < DEPTH)
        def _():
            remote(got.at[k, q], k + 1, q, succ, relay_sem.at[k]).wait_send()

        remote(got.at[k, q], k, q, cross, cross_sem.at[k]).wait_send()
        remote(got.at[k, q], k, q, sib, sib_sem.at[k]).wait_send()
        remote(got.at[k, cross_q], k, cross_q, sib, fwd_sem.at[k]).wait_send()
        return carry

    lax.fori_loop(0, DEPTH, drain, 0)


def fused(ok, kv, q2, win_rows, n_ctx, n_sub):
    rows, hd = q2.shape
    slots = DEPTH * LEVEL
    return pl.pallas_call(
        functools.partial(fused_kernel, n_ctx, n_sub),
        out_shape=jax.ShapeDtypeStruct((rows, hd), q2.dtype),
        in_specs=[
            pl.BlockSpec(memory_space=pltpu.SMEM),
            pl.BlockSpec(memory_space=pltpu.VMEM),
            pl.BlockSpec(memory_space=pltpu.VMEM),
            pl.BlockSpec(memory_space=pltpu.VMEM),
        ],
        out_specs=pl.BlockSpec(memory_space=pltpu.VMEM),
        scratch_shapes=[
            pltpu.VMEM((DEPTH, LEVEL) + kv.shape, kv.dtype),
            pltpu.VMEM((slots, rows, BLK), jnp.float32),
            pltpu.VMEM((rows, BLK), jnp.float32),
            pltpu.VMEM((rows, hd), jnp.float32),
            pltpu.VMEM((rows, BLK), jnp.float32),
            pltpu.SemaphoreType.DMA((DEPTH, LEVEL)),
            pltpu.SemaphoreType.DMA((DEPTH,)),
            pltpu.SemaphoreType.DMA((DEPTH,)),
            pltpu.SemaphoreType.DMA((DEPTH,)),
            pltpu.SemaphoreType.DMA((DEPTH,)),
            pltpu.SemaphoreType.DMA((1,)),
        ],
        compiler_params=pltpu.CompilerParams(
            collective_id=0, has_side_effects=True, vmem_limit_bytes=60 * 1024 * 1024
        ),
    )(ok, kv, q2, win_rows)


def local(queries, key_rows, value_rows, block_docs, windows):
    n_ctx = lax.axis_size("ctx")
    n_sub = lax.axis_size("sub")
    c = lax.axis_index("ctx")
    s = lax.axis_index("sub")
    g = c * n_sub + s
    q = s % LEVEL
    rows_here, heads, hd = queries.shape
    kv = jnp.stack([key_rows, value_rows])

    k_of = jnp.arange(DEPTH * LEVEL, dtype=jnp.int32) // LEVEL
    col_of = jnp.arange(DEPTH * LEVEL, dtype=jnp.int32) % LEVEL
    dist = LEVEL * k_of + q - col_of
    key_block = g - dist
    doc_here = block_docs[g]
    doc_there = jnp.take(block_docs, jnp.clip(key_block, 0, block_docs.shape[0] - 1))
    ok = (dist >= 0) & (dist < WMAX) & (key_block >= 0) & (doc_there == doc_here)
    win_rows = jnp.broadcast_to(jnp.tile(windows, rows_here)[:, None], (rows_here * heads, BLK))
    out = fused(ok.astype(jnp.int32), kv, queries.reshape(rows_here * heads, hd), win_rows, n_ctx, n_sub)
    return out.reshape(rows_here, heads, hd)


def solution(mesh):
    in_specs = (
        P(("ctx", "sub"), None, None),
        P(("ctx", "sub"), None),
        P(("ctx", "sub"), None),
        P(),
        P(),
    )
    out_specs = P(("ctx", "sub"), None, None)
    return jax.shard_map(local, mesh=mesh, in_specs=in_specs, out_specs=out_specs, check_vma=False)
```

```python
import functools

import jax
import jax.numpy as jnp
from jax import lax
from jax.experimental import pallas as pl
from jax.experimental.pallas import tpu as pltpu
from jax.sharding import PartitionSpec as P

BLK = 128
WMAX = 32
LEVEL = 4
DEPTH = (WMAX - 1 + LEVEL - 1) // LEVEL + 1
MESH = pl.DeviceIdType.MESH
CHUNK = 256


def fused_kernel(n_ctx, n_sub, ok_ref, kv_ref, q_ref, win_ref, out_ref,
                 got, s_sc, m_sc, num_sc, den_sc,
                 recv_sem, relay_sem, sib_sem, cross_sem, fwd_sem, own_sem):
    c = lax.axis_index("ctx")
    s = lax.axis_index("sub")
    total = n_ctx * n_sub
    g = c * n_sub + s
    q = s % LEVEL
    succ_g = (g + LEVEL) % total
    pred_g = (g + total - LEVEL) % total
    succ = (succ_g // n_sub, succ_g % n_sub)
    pred = (pred_g // n_sub, pred_g % n_sub)
    sib_q = q + 1 - 2 * (q % 2)
    cross_q = q + 2 - 4 * ((q // 2) % 2)
    far_q = 3 - q
    sib = (c, s - q + sib_q)
    cross = (c, s - q + cross_q)
    rows, hd = q_ref.shape
    heads = rows // BLK
    scale = hd ** -0.5
    n_chunks = rows // CHUNK

    barrier = pltpu.get_barrier_semaphore()
    for peer in (succ, pred, sib, cross):
        pl.semaphore_signal(barrier, inc=1, device_id=peer, device_id_type=MESH)
    pl.semaphore_wait(barrier, 4)

    own = pltpu.make_async_copy(kv_ref, got.at[0, q], own_sem.at[0])
    own.start()

    def remote(src, k, col, peer, sem):
        return pltpu.make_async_remote_copy(
            src_ref=src,
            dst_ref=got.at[k, col],
            send_sem=sem,
            recv_sem=recv_sem.at[k, col],
            device_id=peer,
            device_id_type=MESH,
        )

    m_sc[...] = jnp.full(m_sc.shape, -jnp.inf, jnp.float32)
    win8 = win_ref[...]

    def logits(k, col, causal=False):
        slot = k * LEVEL + col
        d = LEVEL * k + q - col
        live = ok_ref[slot] != 0

        @pl.when((d >= 0) & (d < WMAX) & (g >= d))
        def _():
            allowed = (win8 > d) & live

            def body(ci, carry):
                r0 = pl.multiple_of(ci * CHUNK, CHUNK)
                qc = q_ref[pl.ds(r0, CHUNK), :]
                kb = got[k, col, 0]
                sc = lax.dot_general(qc, kb, (((1,), (1,)), ((), ())), preferred_element_type=jnp.float32) * scale
                sc = sc.reshape(CHUNK // heads, heads, BLK)
                keep = allowed[None]
                if causal:
                    query_i = lax.broadcasted_iota(jnp.int32, sc.shape, 0) + r0 // heads
                    key_j = lax.broadcasted_iota(jnp.int32, sc.shape, 2)
                    keep = keep & (key_j <= query_i)
                sc = jnp.where(keep, sc, -jnp.inf).reshape(CHUNK, BLK)
                s_sc[slot, pl.ds(r0, CHUNK), :] = sc
                m_sc[pl.ds(r0, CHUNK), :] = jnp.maximum(m_sc[pl.ds(r0, CHUNK), :], sc)
                return carry

            lax.fori_loop(0, n_chunks, body, 0)

    remote(kv_ref, 1, q, succ, relay_sem.at[0]).start()
    remote(kv_ref, 0, q, cross, cross_sem.at[0]).start()
    remote(kv_ref, 0, q, sib, sib_sem.at[0]).start()

    def relay_step(k, carry):
        src = got.at[k, q]
        remote(src, k, q, pred, relay_sem.at[k - 1]).wait_recv()

        @pl.when(k + 1 < DEPTH)
        def _():
            remote(src, k + 1, q, succ, relay_sem.at[k]).start()

        remote(src, k, q, cross, cross_sem.at[k]).start()
        remote(src, k, q, sib, sib_sem.at[k]).start()
        return carry

    lax.fori_loop(1, DEPTH, relay_step, 0)

    def cross_step(k, carry):
        src = got.at[k, cross_q]
        remote(src, k, cross_q, cross, cross_sem.at[k]).wait_recv()
        remote(src, k, cross_q, sib, fwd_sem.at[k]).start()
        return carry

    lax.fori_loop(0, DEPTH, cross_step, 0)

    own.wait()
    logits(0, q, causal=True)

    def here_step(k, carry):
        logits(k, q)
        logits(k, cross_q)
        return carry

    lax.fori_loop(1, DEPTH, here_step, 0)
    logits(0, cross_q)

    def sib_step(k, carry):
        remote(got.at[k, sib_q], k, sib_q, sib, sib_sem.at[k]).wait_recv()
        logits(k, sib_q)
        remote(got.at[k, far_q], k, far_q, sib, fwd_sem.at[k]).wait_recv()
        logits(k, far_q)
        return carry

    lax.fori_loop(0, DEPTH, sib_step, 0)

    num_sc[...] = jnp.zeros(num_sc.shape, jnp.float32)
    den_sc[...] = jnp.zeros(den_sc.shape, jnp.float32)

    def weigh_chunk(ci, carry):
        r0 = pl.multiple_of(ci * CHUNK, CHUNK)
        m_sc[pl.ds(r0, CHUNK), :] = jnp.broadcast_to(
            jnp.max(m_sc[pl.ds(r0, CHUNK), :], axis=1, keepdims=True), (CHUNK, BLK)
        )

        def weigh(slot, c2):
            d = LEVEL * (slot // LEVEL) + q - slot % LEVEL

            @pl.when((d >= 0) & (d < WMAX) & (g >= d))
            def _():
                w = jnp.exp(s_sc[slot, pl.ds(r0, CHUNK), :] - m_sc[pl.ds(r0, CHUNK), :]).astype(jnp.bfloat16)
                vb = got[slot // LEVEL, slot % LEVEL, 1]
                num_sc[pl.ds(r0, CHUNK), :] += jnp.dot(w, vb, preferred_element_type=jnp.float32)
                den_sc[pl.ds(r0, CHUNK), :] += w.astype(jnp.float32)

            return c2

        lax.fori_loop(0, DEPTH * LEVEL, weigh, 0)
        den = jnp.sum(den_sc[pl.ds(r0, CHUNK), :], axis=1, keepdims=True)
        out_ref[pl.ds(r0, CHUNK), :] = (num_sc[pl.ds(r0, CHUNK), :] / den).astype(out_ref.dtype)
        return carry

    lax.fori_loop(0, n_chunks, weigh_chunk, 0)

    def drain(k, carry):
        @pl.when(k + 1 < DEPTH)
        def _():
            remote(got.at[k, q], k + 1, q, succ, relay_sem.at[k]).wait_send()

        remote(got.at[k, q], k, q, cross, cross_sem.at[k]).wait_send()
        remote(got.at[k, q], k, q, sib, sib_sem.at[k]).wait_send()
        remote(got.at[k, cross_q], k, cross_q, sib, fwd_sem.at[k]).wait_send()
        return carry

    lax.fori_loop(0, DEPTH, drain, 0)


def fused(ok, kv, q2, win_rows, n_ctx, n_sub):
    rows, hd = q2.shape
    slots = DEPTH * LEVEL
    return pl.pallas_call(
        functools.partial(fused_kernel, n_ctx, n_sub),
        out_shape=jax.ShapeDtypeStruct((rows, hd), q2.dtype),
        in_specs=[
            pl.BlockSpec(memory_space=pltpu.SMEM),
            pl.BlockSpec(memory_space=pltpu.VMEM),
            pl.BlockSpec(memory_space=pltpu.VMEM),
            pl.BlockSpec(memory_space=pltpu.VMEM),
        ],
        out_specs=pl.BlockSpec(memory_space=pltpu.VMEM),
        scratch_shapes=[
            pltpu.VMEM((DEPTH, LEVEL) + kv.shape, kv.dtype),
            pltpu.VMEM((slots, rows, BLK), jnp.float32),
            pltpu.VMEM((rows, BLK), jnp.float32),
            pltpu.VMEM((rows, hd), jnp.float32),
            pltpu.VMEM((rows, BLK), jnp.float32),
            pltpu.SemaphoreType.DMA((DEPTH, LEVEL)),
            pltpu.SemaphoreType.DMA((DEPTH,)),
            pltpu.SemaphoreType.DMA((DEPTH,)),
            pltpu.SemaphoreType.DMA((DEPTH,)),
            pltpu.SemaphoreType.DMA((DEPTH,)),
            pltpu.SemaphoreType.DMA((1,)),
        ],
        compiler_params=pltpu.CompilerParams(
            collective_id=0, has_side_effects=True, vmem_limit_bytes=60 * 1024 * 1024
        ),
    )(ok, kv, q2, win_rows)


def local(queries, key_rows, value_rows, block_docs, windows):
    n_ctx = lax.axis_size("ctx")
    n_sub = lax.axis_size("sub")
    c = lax.axis_index("ctx")
    s = lax.axis_index("sub")
    g = c * n_sub + s
    q = s % LEVEL
    rows_here, heads, hd = queries.shape
    kv = jnp.stack([key_rows, value_rows])

    k_of = jnp.arange(DEPTH * LEVEL, dtype=jnp.int32) // LEVEL
    col_of = jnp.arange(DEPTH * LEVEL, dtype=jnp.int32) % LEVEL
    dist = LEVEL * k_of + q - col_of
    key_block = g - dist
    doc_here = block_docs[g]
    doc_there = jnp.take(block_docs, jnp.clip(key_block, 0, block_docs.shape[0] - 1))
    ok = (dist >= 0) & (dist < WMAX) & (key_block >= 0) & (doc_there == doc_here)
    win_rows = jnp.broadcast_to(windows[:, None], (heads, BLK))
    out = fused(ok.astype(jnp.int32), kv, queries.reshape(rows_here * heads, hd), win_rows, n_ctx, n_sub)
    return out.reshape(rows_here, heads, hd)


def solution(mesh):
    in_specs = (
        P(("ctx", "sub"), None, None),
        P(("ctx", "sub"), None),
        P(("ctx", "sub"), None),
        P(),
        P(),
    )
    out_specs = P(("ctx", "sub"), None, None)
    return jax.shard_map(local, mesh=mesh, in_specs=in_specs, out_specs=out_specs, check_vma=False)
```

```python
import functools

import jax
import jax.numpy as jnp
from jax import lax
from jax.experimental import pallas as pl
from jax.experimental.pallas import tpu as pltpu
from jax.sharding import PartitionSpec as P

BLK = 128
WMAX = 32
LEVEL = 4
DEPTH = (WMAX - 1 + LEVEL - 1) // LEVEL + 1
MESH = pl.DeviceIdType.MESH


def relay_kernel(n_ctx, n_sub, kv_ref, got_ref, recv_sem, relay_sem, sib_sem, cross_sem, fwd_sem, own_sem):
    c = lax.axis_index("ctx")
    s = lax.axis_index("sub")
    total = n_ctx * n_sub
    g = c * n_sub + s
    q = s % LEVEL
    succ_g = (g + LEVEL) % total
    pred_g = (g + total - LEVEL) % total
    succ = (succ_g // n_sub, succ_g % n_sub)
    pred = (pred_g // n_sub, pred_g % n_sub)
    sib_q = q + 1 - 2 * (q % 2)
    cross_q = q + 2 - 4 * ((q // 2) % 2)
    sib = (c, s - q + sib_q)
    cross = (c, s - q + cross_q)

    barrier = pltpu.get_barrier_semaphore()
    for peer in (succ, pred, sib, cross):
        pl.semaphore_signal(barrier, inc=1, device_id=peer, device_id_type=MESH)
    pl.semaphore_wait(barrier, 4)

    own = pltpu.make_async_copy(kv_ref, got_ref.at[0, q], own_sem.at[0])
    own.start()

    def remote(src, k, col, peer, sem):
        return pltpu.make_async_remote_copy(
            src_ref=src,
            dst_ref=got_ref.at[k, col],
            send_sem=sem,
            recv_sem=recv_sem.at[k, col],
            device_id=peer,
            device_id_type=MESH,
        )

    sends = []
    for k in range(DEPTH):
        src = kv_ref if k == 0 else got_ref.at[k, q]
        if k > 0:
            remote(src, k, q, pred, relay_sem.at[k - 1]).wait_recv()
        if k + 1 < DEPTH:
            cp = remote(src, k + 1, q, succ, relay_sem.at[k])
            cp.start()
            sends.append(cp)
        cp = remote(src, k, q, cross, cross_sem.at[k])
        cp.start()
        sends.append(cp)
        cp = remote(src, k, q, sib, sib_sem.at[k])
        cp.start()
        sends.append(cp)

    for k in range(DEPTH):
        got_cross = got_ref.at[k, cross_q]
        remote(got_cross, k, cross_q, cross, cross_sem.at[k]).wait_recv()
        cp = remote(got_cross, k, cross_q, sib, fwd_sem.at[k])
        cp.start()
        sends.append(cp)

    far_q = 3 - q
    for k in range(DEPTH):
        remote(got_ref.at[k, sib_q], k, sib_q, sib, sib_sem.at[k]).wait_recv()
        remote(got_ref.at[k, far_q], k, far_q, sib, fwd_sem.at[k]).wait_recv()
    for cp in sends:
        cp.wait_send()
    own.wait()


def relay(kv, n_ctx, n_sub):
    return pl.pallas_call(
        functools.partial(relay_kernel, n_ctx, n_sub),
        out_shape=jax.ShapeDtypeStruct((DEPTH, LEVEL) + kv.shape, kv.dtype),
        in_specs=[pl.BlockSpec(memory_space=pltpu.VMEM)],
        out_specs=pl.BlockSpec(memory_space=pl.ANY),
        scratch_shapes=[
            pltpu.SemaphoreType.DMA((DEPTH, LEVEL)),
            pltpu.SemaphoreType.DMA((DEPTH,)),
            pltpu.SemaphoreType.DMA((DEPTH,)),
            pltpu.SemaphoreType.DMA((DEPTH,)),
            pltpu.SemaphoreType.DMA((DEPTH,)),
            pltpu.SemaphoreType.DMA((1,)),
        ],
        compiler_params=pltpu.CompilerParams(collective_id=0, has_side_effects=True),
    )(kv)


def attend_kernel(q_ref, k_ref, v_ref, bias_ref, own_ref, out_ref, s_sc):
    rows, hd = q_ref.shape
    chunk, keys = s_sc.shape
    heads = bias_ref.shape[0]
    scale = hd ** -0.5
    own = pl.multiple_of(own_ref[0] * BLK, BLK)
    ones = jnp.ones((keys, BLK), jnp.bfloat16)

    def one_chunk(ci, carry):
        r0 = pl.multiple_of(ci * chunk, chunk)
        qc = q_ref[pl.ds(r0, chunk), :]
        sc = lax.dot_general(qc, k_ref[...], (((1,), (1,)), ((), ())), preferred_element_type=jnp.float32) * scale
        sc = (sc.reshape(chunk // heads, heads, keys) + bias_ref[...][None]).reshape(chunk, keys)
        s_sc[...] = sc
        query_i = (lax.broadcasted_iota(jnp.int32, (chunk, BLK), 0) + r0) // heads
        key_j = lax.broadcasted_iota(jnp.int32, (chunk, BLK), 1)
        s_sc[:, pl.ds(own, BLK)] = jnp.where(key_j <= query_i, s_sc[:, pl.ds(own, BLK)], -jnp.inf)
        sc = s_sc[...]
        m = jnp.max(sc, axis=1, keepdims=True)
        w = jnp.exp(sc - m).astype(jnp.bfloat16)
        num = jnp.dot(w, v_ref[...], preferred_element_type=jnp.float32)
        den = jnp.dot(w, ones, preferred_element_type=jnp.float32)
        out_ref[pl.ds(r0, chunk), :] = (num / den[:, :1]).astype(out_ref.dtype)
        return carry

    lax.fori_loop(0, rows // chunk, one_chunk, 0)


def attend(q2, k_all, v_all, bias, own):
    rows, hd = q2.shape
    keys = k_all.shape[0]
    chunk = 256
    return pl.pallas_call(
        attend_kernel,
        out_shape=jax.ShapeDtypeStruct((rows, hd), q2.dtype),
        in_specs=[
            pl.BlockSpec(memory_space=pltpu.VMEM),
            pl.BlockSpec(memory_space=pltpu.VMEM),
            pl.BlockSpec(memory_space=pltpu.VMEM),
            pl.BlockSpec(memory_space=pltpu.VMEM),
            pl.BlockSpec(memory_space=pltpu.SMEM),
        ],
        out_specs=pl.BlockSpec(memory_space=pltpu.VMEM),
        scratch_shapes=[pltpu.VMEM((chunk, keys), jnp.float32)],
        compiler_params=pltpu.CompilerParams(vmem_limit_bytes=48 * 1024 * 1024),
    )(q2, k_all, v_all, bias, own)


def local(queries, key_rows, value_rows, block_docs, windows):
    n_ctx = lax.axis_size("ctx")
    n_sub = lax.axis_size("sub")
    c = lax.axis_index("ctx")
    s = lax.axis_index("sub")
    g = c * n_sub + s
    q = s % LEVEL
    rows_here, heads, hd = queries.shape
    kv = jnp.stack([key_rows, value_rows])
    got = relay(kv, n_ctx, n_sub)
    slots = DEPTH * LEVEL
    k_all = got[:, :, 0].reshape(slots * BLK, hd)
    v_all = got[:, :, 1].reshape(slots * BLK, hd)

    k_of = jnp.arange(slots, dtype=jnp.int32) // LEVEL
    col_of = jnp.arange(slots, dtype=jnp.int32) % LEVEL
    dist = LEVEL * k_of + q - col_of
    key_block = g - dist
    doc_here = block_docs[g]
    doc_there = jnp.take(block_docs, jnp.clip(key_block, 0, block_docs.shape[0] - 1))
    ok = (dist >= 0) & (dist < WMAX) & (key_block >= 0) & (doc_there == doc_here)
    allowed = ok[None, :] & (windows[:, None] > dist[None, :])
    bias = jnp.repeat(jnp.where(allowed, 0.0, -jnp.inf).astype(jnp.float32), BLK, axis=1)
    own = jnp.reshape(q, (1,)).astype(jnp.int32)
    out = attend(queries.reshape(rows_here * heads, hd), k_all, v_all, bias, own)
    return out.reshape(rows_here, heads, hd)


def solution(mesh):
    in_specs = (
        P(("ctx", "sub"), None, None),
        P(("ctx", "sub"), None),
        P(("ctx", "sub"), None),
        P(),
        P(),
    )
    out_specs = P(("ctx", "sub"), None, None)
    return jax.shard_map(local, mesh=mesh, in_specs=in_specs, out_specs=out_specs, check_vma=False)
```

```python
import functools

import jax
import jax.numpy as jnp
from jax import lax
from jax.experimental import pallas as pl
from jax.experimental.pallas import tpu as pltpu
from jax.sharding import PartitionSpec as P

BLK = 128
WMAX = 32
LEVEL = 4
DEPTH = (WMAX - 1 + LEVEL - 1) // LEVEL + 1
MESH = pl.DeviceIdType.MESH


def relay_kernel(n_ctx, n_sub, k_ref, v_ref, got_k, got_v, recv_sem, relay_sem, sib_sem, cross_sem, fwd_sem, own_sem):
    c = lax.axis_index("ctx")
    s = lax.axis_index("sub")
    total = n_ctx * n_sub
    g = c * n_sub + s
    q = s % LEVEL
    succ_g = (g + LEVEL) % total
    pred_g = (g + total - LEVEL) % total
    succ = (succ_g // n_sub, succ_g % n_sub)
    pred = (pred_g // n_sub, pred_g % n_sub)
    sib_q = q + 1 - 2 * (q % 2)
    cross_q = q + 2 - 4 * ((q // 2) % 2)
    far_q = 3 - q
    sib = (c, s - q + sib_q)
    cross = (c, s - q + cross_q)
    planes = (got_k, got_v)
    inputs = (k_ref, v_ref)

    barrier = pltpu.get_barrier_semaphore()
    for peer in (succ, pred, sib, cross):
        pl.semaphore_signal(barrier, inc=1, device_id=peer, device_id_type=MESH)
    pl.semaphore_wait(barrier, 4)

    owns = [pltpu.make_async_copy(inputs[p], planes[p].at[0, q], own_sem.at[p]) for p in range(2)]
    for cp in owns:
        cp.start()

    def remote(p, src, k, col, peer, sem):
        return pltpu.make_async_remote_copy(
            src_ref=src,
            dst_ref=planes[p].at[k, col],
            send_sem=sem.at[p],
            recv_sem=recv_sem.at[p, k, col],
            device_id=peer,
            device_id_type=MESH,
        )

    def source(p, k, col):
        return inputs[p] if k == 0 else planes[p].at[k, col]

    sends = []
    for k in range(DEPTH):
        if k > 0:
            for p in range(2):
                remote(p, source(p, k, q), k, q, pred, relay_sem.at[k - 1]).wait_recv()
        if k + 1 < DEPTH:
            for p in range(2):
                cp = remote(p, source(p, k, q), k + 1, q, succ, relay_sem.at[k])
                cp.start()
                sends.append(cp)
        for p in range(2):
            cp = remote(p, source(p, k, q), k, q, cross, cross_sem.at[k])
            cp.start()
            sends.append(cp)
        for p in range(2):
            cp = remote(p, source(p, k, q), k, q, sib, sib_sem.at[k])
            cp.start()
            sends.append(cp)

    for k in range(DEPTH):
        for p in range(2):
            got_cross = planes[p].at[k, cross_q]
            remote(p, got_cross, k, cross_q, cross, cross_sem.at[k]).wait_recv()
            cp = remote(p, got_cross, k, cross_q, sib, fwd_sem.at[k])
            cp.start()
            sends.append(cp)

    for k in range(DEPTH):
        for p in range(2):
            remote(p, planes[p].at[k, sib_q], k, sib_q, sib, sib_sem.at[k]).wait_recv()
        for p in range(2):
            remote(p, planes[p].at[k, far_q], k, far_q, sib, fwd_sem.at[k]).wait_recv()
    for cp in sends:
        cp.wait_send()
    for cp in owns:
        cp.wait()


def relay(key_rows, value_rows, n_ctx, n_sub):
    plane = jax.ShapeDtypeStruct((DEPTH, LEVEL) + key_rows.shape, key_rows.dtype)
    return pl.pallas_call(
        functools.partial(relay_kernel, n_ctx, n_sub),
        out_shape=(plane, plane),
        in_specs=[pl.BlockSpec(memory_space=pltpu.VMEM)] * 2,
        out_specs=(pl.BlockSpec(memory_space=pl.ANY), pl.BlockSpec(memory_space=pl.ANY)),
        scratch_shapes=[
            pltpu.SemaphoreType.DMA((2, DEPTH, LEVEL)),
            pltpu.SemaphoreType.DMA((DEPTH, 2)),
            pltpu.SemaphoreType.DMA((DEPTH, 2)),
            pltpu.SemaphoreType.DMA((DEPTH, 2)),
            pltpu.SemaphoreType.DMA((DEPTH, 2)),
            pltpu.SemaphoreType.DMA((2,)),
        ],
        compiler_params=pltpu.CompilerParams(collective_id=0, has_side_effects=True),
    )(key_rows, value_rows)


def attend_kernel(q_ref, k_ref, v_ref, bias_ref, own_ref, out_ref, s_sc):
    rows, hd = q_ref.shape
    chunk, keys = s_sc.shape
    heads = bias_ref.shape[0]
    scale = hd ** -0.5
    own = pl.multiple_of(own_ref[0] * BLK, BLK)
    ones = jnp.ones((keys, BLK), jnp.bfloat16)

    def one_chunk(ci, carry):
        r0 = pl.multiple_of(ci * chunk, chunk)
        qc = q_ref[pl.ds(r0, chunk), :]
        sc = lax.dot_general(qc, k_ref[...], (((1,), (1,)), ((), ())), preferred_element_type=jnp.float32) * scale
        sc = (sc.reshape(chunk // heads, heads, keys) + bias_ref[...][None]).reshape(chunk, keys)
        s_sc[...] = sc
        query_i = (lax.broadcasted_iota(jnp.int32, (chunk, BLK), 0) + r0) // heads
        key_j = lax.broadcasted_iota(jnp.int32, (chunk, BLK), 1)
        s_sc[:, pl.ds(own, BLK)] = jnp.where(key_j <= query_i, s_sc[:, pl.ds(own, BLK)], -jnp.inf)
        sc = s_sc[...]
        m = jnp.max(sc, axis=1, keepdims=True)
        w = jnp.exp(sc - m).astype(jnp.bfloat16)
        num = jnp.dot(w, v_ref[...], preferred_element_type=jnp.float32)
        den = jnp.dot(w, ones, preferred_element_type=jnp.float32)
        out_ref[pl.ds(r0, chunk), :] = (num / den[:, :1]).astype(out_ref.dtype)
        return carry

    lax.fori_loop(0, rows // chunk, one_chunk, 0)


def attend(q2, k_all, v_all, bias, own):
    rows, hd = q2.shape
    keys = k_all.shape[0]
    chunk = 256
    return pl.pallas_call(
        attend_kernel,
        out_shape=jax.ShapeDtypeStruct((rows, hd), q2.dtype),
        in_specs=[
            pl.BlockSpec(memory_space=pltpu.VMEM),
            pl.BlockSpec(memory_space=pltpu.VMEM),
            pl.BlockSpec(memory_space=pltpu.VMEM),
            pl.BlockSpec(memory_space=pltpu.VMEM),
            pl.BlockSpec(memory_space=pltpu.SMEM),
        ],
        out_specs=pl.BlockSpec(memory_space=pltpu.VMEM),
        scratch_shapes=[pltpu.VMEM((chunk, keys), jnp.float32)],
        compiler_params=pltpu.CompilerParams(vmem_limit_bytes=48 * 1024 * 1024),
    )(q2, k_all, v_all, bias, own)


def local(queries, key_rows, value_rows, block_docs, windows):
    n_ctx = lax.axis_size("ctx")
    n_sub = lax.axis_size("sub")
    c = lax.axis_index("ctx")
    s = lax.axis_index("sub")
    g = c * n_sub + s
    q = s % LEVEL
    rows_here, heads, hd = queries.shape
    got_k, got_v = relay(key_rows, value_rows, n_ctx, n_sub)
    slots = DEPTH * LEVEL
    k_all = got_k.reshape(slots * BLK, hd)
    v_all = got_v.reshape(slots * BLK, hd)

    k_of = jnp.arange(slots, dtype=jnp.int32) // LEVEL
    col_of = jnp.arange(slots, dtype=jnp.int32) % LEVEL
    dist = LEVEL * k_of + q - col_of
    key_block = g - dist
    doc_here = block_docs[g]
    doc_there = jnp.take(block_docs, jnp.clip(key_block, 0, block_docs.shape[0] - 1))
    ok = (dist >= 0) & (dist < WMAX) & (key_block >= 0) & (doc_there == doc_here)
    allowed = ok[None, :] & (windows[:, None] > dist[None, :])
    bias = jnp.repeat(jnp.where(allowed, 0.0, -jnp.inf).astype(jnp.float32), BLK, axis=1)
    own = jnp.reshape(q, (1,)).astype(jnp.int32)
    out = attend(queries.reshape(rows_here * heads, hd), k_all, v_all, bias, own)
    return out.reshape(rows_here, heads, hd)


def solution(mesh):
    in_specs = (
        P(("ctx", "sub"), None, None),
        P(("ctx", "sub"), None),
        P(("ctx", "sub"), None),
        P(),
        P(),
    )
    out_specs = P(("ctx", "sub"), None, None)
    return jax.shard_map(local, mesh=mesh, in_specs=in_specs, out_specs=out_specs, check_vma=False)
```

```python
import functools

import jax
import jax.numpy as jnp
from jax import lax
from jax.experimental import pallas as pl
from jax.experimental.pallas import tpu as pltpu
from jax.sharding import PartitionSpec as P

BLK = 128
WMAX = 32
LEVEL = 4
DEPTH = (WMAX - 1 + LEVEL - 1) // LEVEL + 1
MESH = pl.DeviceIdType.MESH


def fused_kernel(n_ctx, n_sub, docs_ref, win_ref, k_ref, v_ref, q_ref, out_ref,
                 got_k, got_v, bias_sc, s_sc, recv_sem, relay_sem, sib_sem, cross_sem, fwd_sem, own_sem):
    c = lax.axis_index("ctx")
    s = lax.axis_index("sub")
    total = n_ctx * n_sub
    g = c * n_sub + s
    q = s % LEVEL
    succ_g = (g + LEVEL) % total
    pred_g = (g + total - LEVEL) % total
    succ = (succ_g // n_sub, succ_g % n_sub)
    pred = (pred_g // n_sub, pred_g % n_sub)
    sib_q = q + 1 - 2 * (q % 2)
    cross_q = q + 2 - 4 * ((q // 2) % 2)
    far_q = 3 - q
    sib = (c, s - q + sib_q)
    cross = (c, s - q + cross_q)
    planes = (got_k, got_v)
    inputs = (k_ref, v_ref)
    rows, hd = q_ref.shape
    chunk, keys = s_sc.shape
    heads = bias_sc.shape[0]
    n_blocks = docs_ref.shape[0]

    def at(p, k, col):
        return planes[p].at[pl.ds(pl.multiple_of((k * LEVEL + col) * BLK, BLK), BLK)]

    barrier = pltpu.get_barrier_semaphore()
    for peer in (succ, pred, sib, cross):
        pl.semaphore_signal(barrier, inc=1, device_id=peer, device_id_type=MESH)
    pl.semaphore_wait(barrier, 4)

    owns = [pltpu.make_async_copy(inputs[p], at(p, 0, q), own_sem.at[p]) for p in range(2)]
    for cp in owns:
        cp.start()

    def remote(p, src, k, col, peer, sem):
        return pltpu.make_async_remote_copy(
            src_ref=src,
            dst_ref=at(p, k, col),
            send_sem=sem.at[p],
            recv_sem=recv_sem.at[p, k, col],
            device_id=peer,
            device_id_type=MESH,
        )

    def source(p, k, col):
        return inputs[p] if k == 0 else at(p, k, col)

    sends = []
    for k in range(DEPTH):
        if k > 0:
            for p in range(2):
                remote(p, source(p, k, q), k, q, pred, relay_sem.at[k - 1]).wait_recv()
        if k + 1 < DEPTH:
            for p in range(2):
                cp = remote(p, source(p, k, q), k + 1, q, succ, relay_sem.at[k])
                cp.start()
                sends.append(cp)
        for p in range(2):
            cp = remote(p, source(p, k, q), k, q, cross, cross_sem.at[k])
            cp.start()
            sends.append(cp)
        for p in range(2):
            cp = remote(p, source(p, k, q), k, q, sib, sib_sem.at[k])
            cp.start()
            sends.append(cp)
        if k == 0:
            head = lax.broadcasted_iota(jnp.int32, (heads, BLK), 0)
            win8 = jnp.zeros((heads, BLK), jnp.int32)
            for h in range(heads):
                win8 = jnp.where(head == h, win_ref[h], win8)
            doc_here = docs_ref[g]
            for slot in range(DEPTH * LEVEL):
                d = LEVEL * (slot // LEVEL) + q - slot % LEVEL
                kb = g - d
                doc_there = docs_ref[(kb + n_blocks) % n_blocks]
                live = (d >= 0) & (d < WMAX) & (kb >= 0) & (doc_there == doc_here)
                keep = (win8 > d) & (jnp.full((heads, BLK), live.astype(jnp.int32)) > 0)
                bias_sc[:, pl.ds(slot * BLK, BLK)] = jnp.where(keep, 0.0, -jnp.inf).astype(jnp.float32)

    for k in range(DEPTH):
        for p in range(2):
            got_cross = at(p, k, cross_q)
            remote(p, got_cross, k, cross_q, cross, cross_sem.at[k]).wait_recv()
            cp = remote(p, got_cross, k, cross_q, sib, fwd_sem.at[k])
            cp.start()
            sends.append(cp)

    for k in range(DEPTH):
        for p in range(2):
            remote(p, at(p, k, sib_q), k, sib_q, sib, sib_sem.at[k]).wait_recv()
        for p in range(2):
            remote(p, at(p, k, far_q), k, far_q, sib, fwd_sem.at[k]).wait_recv()
    for cp in owns:
        cp.wait()

    scale = hd ** -0.5
    own = pl.multiple_of(q * BLK, BLK)
    ones = jnp.ones((keys, BLK), jnp.bfloat16)

    def one_chunk(ci, carry):
        r0 = pl.multiple_of(ci * chunk, chunk)
        qc = q_ref[pl.ds(r0, chunk), :]
        sc = lax.dot_general(qc, got_k[...], (((1,), (1,)), ((), ())), preferred_element_type=jnp.float32) * scale
        sc = (sc.reshape(chunk // heads, heads, keys) + bias_sc[...][None]).reshape(chunk, keys)
        s_sc[...] = sc
        query_i = (lax.broadcasted_iota(jnp.int32, (chunk, BLK), 0) + r0) // heads
        key_j = lax.broadcasted_iota(jnp.int32, (chunk, BLK), 1)
        s_sc[:, pl.ds(own, BLK)] = jnp.where(key_j <= query_i, s_sc[:, pl.ds(own, BLK)], -jnp.inf)
        sc = s_sc[...]
        m = jnp.max(sc, axis=1, keepdims=True)
        w = jnp.exp(sc - m).astype(jnp.bfloat16)
        num = jnp.dot(w, got_v[...], preferred_element_type=jnp.float32)
        den = jnp.dot(w, ones, preferred_element_type=jnp.float32)
        out_ref[pl.ds(r0, chunk), :] = (num / den[:, :1]).astype(out_ref.dtype)
        return carry

    lax.fori_loop(0, rows // chunk, one_chunk, 0)

    for cp in sends:
        cp.wait_send()


def fused(block_docs, windows, key_rows, value_rows, q2, n_ctx, n_sub):
    rows, hd = q2.shape
    keys = DEPTH * LEVEL * BLK
    chunk = 256
    heads = windows.shape[0]
    return pl.pallas_call(
        functools.partial(fused_kernel, n_ctx, n_sub),
        out_shape=jax.ShapeDtypeStruct((rows, hd), q2.dtype),
        in_specs=[
            pl.BlockSpec(memory_space=pltpu.SMEM),
            pl.BlockSpec(memory_space=pltpu.SMEM),
            pl.BlockSpec(memory_space=pltpu.VMEM),
            pl.BlockSpec(memory_space=pltpu.VMEM),
            pl.BlockSpec(memory_space=pltpu.VMEM),
        ],
        out_specs=pl.BlockSpec(memory_space=pltpu.VMEM),
        scratch_shapes=[
            pltpu.VMEM((keys, hd), key_rows.dtype),
            pltpu.VMEM((keys, hd), value_rows.dtype),
            pltpu.VMEM((heads, keys), jnp.float32),
            pltpu.VMEM((chunk, keys), jnp.float32),
            pltpu.SemaphoreType.DMA((2, DEPTH, LEVEL)),
            pltpu.SemaphoreType.DMA((DEPTH, 2)),
            pltpu.SemaphoreType.DMA((DEPTH, 2)),
            pltpu.SemaphoreType.DMA((DEPTH, 2)),
            pltpu.SemaphoreType.DMA((DEPTH, 2)),
            pltpu.SemaphoreType.DMA((2,)),
        ],
        compiler_params=pltpu.CompilerParams(
            collective_id=0, has_side_effects=True, vmem_limit_bytes=48 * 1024 * 1024
        ),
    )(block_docs, windows, key_rows, value_rows, q2)


def local(queries, key_rows, value_rows, block_docs, windows):
    n_ctx = lax.axis_size("ctx")
    n_sub = lax.axis_size("sub")
    rows_here, heads, hd = queries.shape
    out = fused(block_docs, windows, key_rows, value_rows, queries.reshape(rows_here * heads, hd), n_ctx, n_sub)
    return out.reshape(rows_here, heads, hd)


def solution(mesh):
    in_specs = (
        P(("ctx", "sub"), None, None),
        P(("ctx", "sub"), None),
        P(("ctx", "sub"), None),
        P(),
        P(),
    )
    out_specs = P(("ctx", "sub"), None, None)
    return jax.shard_map(local, mesh=mesh, in_specs=in_specs, out_specs=out_specs, check_vma=False)
```

```python
import functools

import jax
import jax.numpy as jnp
from jax import lax
from jax.experimental import pallas as pl
from jax.experimental.pallas import tpu as pltpu
from jax.sharding import PartitionSpec as P

BLK = 128
WMAX = 32
LEVEL = 4
DEPTH = (WMAX - 1 + LEVEL - 1) // LEVEL + 1
MESH = pl.DeviceIdType.MESH


def fused_kernel(n_ctx, n_sub, docs_hbm, win_hbm, k_ref, v_ref, q_hbm, out_ref,
                 got_k, got_v, bias_sc, s_sc, q_ref, docs_ref, win_ref, in_sem,
                 recv_sem, relay_sem, sib_sem, cross_sem, fwd_sem, own_sem):
    c = lax.axis_index("ctx")
    s = lax.axis_index("sub")
    total = n_ctx * n_sub
    g = c * n_sub + s
    q = s % LEVEL
    succ_g = (g + LEVEL) % total
    pred_g = (g + total - LEVEL) % total
    succ = (succ_g // n_sub, succ_g % n_sub)
    pred = (pred_g // n_sub, pred_g % n_sub)
    sib_q = q + 1 - 2 * (q % 2)
    cross_q = q + 2 - 4 * ((q // 2) % 2)
    far_q = 3 - q
    sib = (c, s - q + sib_q)
    cross = (c, s - q + cross_q)
    planes = (got_k, got_v)
    inputs = (k_ref, v_ref)
    rows, hd = q_ref.shape
    chunk, keys = s_sc.shape
    heads = bias_sc.shape[0]
    n_blocks = docs_ref.shape[0]

    def at(p, k, col):
        return planes[p].at[pl.ds(pl.multiple_of((k * LEVEL + col) * BLK, BLK), BLK)]

    loads = [
        pltpu.make_async_copy(docs_hbm, docs_ref, in_sem.at[0]),
        pltpu.make_async_copy(win_hbm, win_ref, in_sem.at[1]),
        pltpu.make_async_copy(q_hbm, q_ref, in_sem.at[2]),
    ]
    for cp in loads:
        cp.start()

    barrier = pltpu.get_barrier_semaphore()
    for peer in (succ, pred, sib, cross):
        pl.semaphore_signal(barrier, inc=1, device_id=peer, device_id_type=MESH)
    pl.semaphore_wait(barrier, 4)

    owns = [pltpu.make_async_copy(inputs[p], at(p, 0, q), own_sem.at[p]) for p in range(2)]
    for cp in owns:
        cp.start()

    def remote(p, src, k, col, peer, sem):
        return pltpu.make_async_remote_copy(
            src_ref=src,
            dst_ref=at(p, k, col),
            send_sem=sem.at[p],
            recv_sem=recv_sem.at[p, k, col],
            device_id=peer,
            device_id_type=MESH,
        )

    def source(p, k, col):
        return inputs[p] if k == 0 else at(p, k, col)

    sends = []
    for k in range(DEPTH):
        if k > 0:
            for p in range(2):
                remote(p, source(p, k, q), k, q, pred, relay_sem.at[k - 1]).wait_recv()
        if k + 1 < DEPTH:
            for p in range(2):
                cp = remote(p, source(p, k, q), k + 1, q, succ, relay_sem.at[k])
                cp.start()
                sends.append(cp)
        for p in range(2):
            cp = remote(p, source(p, k, q), k, q, cross, cross_sem.at[k])
            cp.start()
            sends.append(cp)
        for p in range(2):
            cp = remote(p, source(p, k, q), k, q, sib, sib_sem.at[k])
            cp.start()
            sends.append(cp)
        if k == 0:
            loads[0].wait()
            loads[1].wait()
            head = lax.broadcasted_iota(jnp.int32, (heads, BLK), 0)
            win8 = jnp.zeros((heads, BLK), jnp.int32)
            for h in range(heads):
                win8 = jnp.where(head == h, win_ref[h], win8)
            doc_here = docs_ref[g]
            for slot in range(DEPTH * LEVEL):
                d = LEVEL * (slot // LEVEL) + q - slot % LEVEL
                kb = g - d
                doc_there = docs_ref[(kb + n_blocks) % n_blocks]
                live = (d >= 0) & (d < WMAX) & (kb >= 0) & (doc_there == doc_here)
                keep = (win8 > d) & (jnp.full((heads, BLK), live.astype(jnp.int32)) > 0)
                bias_sc[:, pl.ds(slot * BLK, BLK)] = jnp.where(keep, 0.0, -jnp.inf).astype(jnp.float32)

    for k in range(DEPTH):
        for p in range(2):
            got_cross = at(p, k, cross_q)
            remote(p, got_cross, k, cross_q, cross, cross_sem.at[k]).wait_recv()
            cp = remote(p, got_cross, k, cross_q, sib, fwd_sem.at[k])
            cp.start()
            sends.append(cp)

    for k in range(DEPTH):
        for p in range(2):
            remote(p, at(p, k, sib_q), k, sib_q, sib, sib_sem.at[k]).wait_recv()
        for p in range(2):
            remote(p, at(p, k, far_q), k, far_q, sib, fwd_sem.at[k]).wait_recv()
    for cp in owns:
        cp.wait()
    loads[2].wait()

    scale = hd ** -0.5
    own = pl.multiple_of(q * BLK, BLK)
    ones = jnp.ones((keys, BLK), jnp.bfloat16)

    def one_chunk(ci, carry):
        r0 = pl.multiple_of(ci * chunk, chunk)
        qc = q_ref[pl.ds(r0, chunk), :]
        sc = lax.dot_general(qc, got_k[...], (((1,), (1,)), ((), ())), preferred_element_type=jnp.float32) * scale
        sc = (sc.reshape(chunk // heads, heads, keys) + bias_sc[...][None]).reshape(chunk, keys)
        s_sc[...] = sc
        query_i = (lax.broadcasted_iota(jnp.int32, (chunk, BLK), 0) + r0) // heads
        key_j = lax.broadcasted_iota(jnp.int32, (chunk, BLK), 1)
        s_sc[:, pl.ds(own, BLK)] = jnp.where(key_j <= query_i, s_sc[:, pl.ds(own, BLK)], -jnp.inf)
        sc = s_sc[...]
        m = jnp.max(sc, axis=1, keepdims=True)
        w = jnp.exp(sc - m).astype(jnp.bfloat16)
        num = jnp.dot(w, got_v[...], preferred_element_type=jnp.float32)
        den = jnp.dot(w, ones, preferred_element_type=jnp.float32)
        out_ref[pl.ds(r0, chunk), :] = (num / den[:, :1]).astype(out_ref.dtype)
        return carry

    lax.fori_loop(0, rows // chunk, one_chunk, 0)

    for cp in sends:
        cp.wait_send()


def fused(block_docs, windows, key_rows, value_rows, q2, n_ctx, n_sub):
    rows, hd = q2.shape
    keys = DEPTH * LEVEL * BLK
    chunk = 256
    heads = windows.shape[0]
    return pl.pallas_call(
        functools.partial(fused_kernel, n_ctx, n_sub),
        out_shape=jax.ShapeDtypeStruct((rows, hd), q2.dtype),
        in_specs=[pl.BlockSpec(memory_space=pltpu.HBM)] * 5,
        out_specs=pl.BlockSpec(memory_space=pltpu.VMEM),
        scratch_shapes=[
            pltpu.VMEM((keys, hd), key_rows.dtype),
            pltpu.VMEM((keys, hd), value_rows.dtype),
            pltpu.VMEM((heads, keys), jnp.float32),
            pltpu.VMEM((chunk, keys), jnp.float32),
            pltpu.VMEM((rows, hd), q2.dtype),
            pltpu.SMEM(block_docs.shape, jnp.int32),
            pltpu.SMEM(windows.shape, jnp.int32),
            pltpu.SemaphoreType.DMA((3,)),
            pltpu.SemaphoreType.DMA((2, DEPTH, LEVEL)),
            pltpu.SemaphoreType.DMA((DEPTH, 2)),
            pltpu.SemaphoreType.DMA((DEPTH, 2)),
            pltpu.SemaphoreType.DMA((DEPTH, 2)),
            pltpu.SemaphoreType.DMA((DEPTH, 2)),
            pltpu.SemaphoreType.DMA((2,)),
        ],
        compiler_params=pltpu.CompilerParams(
            collective_id=0, has_side_effects=True, vmem_limit_bytes=67043328
        ),
    )(block_docs, windows, key_rows, value_rows, q2)


def local(queries, key_rows, value_rows, block_docs, windows):
    n_ctx = lax.axis_size("ctx")
    n_sub = lax.axis_size("sub")
    rows_here, heads, hd = queries.shape
    out = fused(block_docs, windows, key_rows, value_rows, queries.reshape(rows_here * heads, hd), n_ctx, n_sub)
    return out.reshape(rows_here, heads, hd)


def solution(mesh):
    in_specs = (
        P(("ctx", "sub"), None, None),
        P(("ctx", "sub"), None),
        P(("ctx", "sub"), None),
        P(),
        P(),
    )
    out_specs = P(("ctx", "sub"), None, None)
    return jax.shard_map(local, mesh=mesh, in_specs=in_specs, out_specs=out_specs, check_vma=False)
```

```python
import functools

import jax
import jax.numpy as jnp
from jax import lax
from jax.experimental import pallas as pl
from jax.experimental.pallas import tpu as pltpu
from jax.sharding import PartitionSpec as P

BLK = 128
WMAX = 32
LEVEL = 4
DEPTH = (WMAX - 1 + LEVEL - 1) // LEVEL + 1
MESH = pl.DeviceIdType.MESH


def fused_kernel(n_ctx, n_sub, docs_hbm, win_hbm, k_ref, v_ref, q_hbm, out_ref,
                 got_k, got_v, bias_sc, s_sc, q_ref, docs_ref, win_ref, in_sem,
                 recv_sem, relay_sem, sib_sem, cross_sem, fwd_sem, own_sem,
                 hop_k, hop_v, hop_sem, onward_sem):
    c = lax.axis_index("ctx")
    s = lax.axis_index("sub")
    total = n_ctx * n_sub
    g = c * n_sub + s
    q = s % LEVEL
    succ_g = (g + LEVEL) % total
    pred_g = (g + total - LEVEL) % total
    succ = (succ_g // n_sub, succ_g % n_sub)
    pred = (pred_g // n_sub, pred_g % n_sub)
    sib_q = q + 1 - 2 * (q % 2)
    cross_q = q + 2 - 4 * ((q // 2) % 2)
    far_q = 3 - q
    sib = (c, s - q + sib_q)
    cross = (c, s - q + cross_q)
    z = s // LEVEL
    last_z = n_sub // LEVEL - 1
    first = z == 0
    last = z == last_z
    next_c = (c + 1) % n_ctx
    prev_c = (c + n_ctx - 1) % n_ctx
    last_here = (c, last_z * LEVEL + q)
    first_here = (c, q)
    last_next = (next_c, last_z * LEVEL + q)
    last_prev = (prev_c, last_z * LEVEL + q)
    first_next = (next_c, q)
    first_prev = (prev_c, q)
    hops = (hop_k, hop_v)
    planes = (got_k, got_v)
    inputs = (k_ref, v_ref)
    rows, hd = q_ref.shape
    chunk, keys = s_sc.shape
    heads = bias_sc.shape[0]
    n_blocks = docs_ref.shape[0]

    def at(p, k, col):
        return planes[p].at[pl.ds(pl.multiple_of((k * LEVEL + col) * BLK, BLK), BLK)]

    loads = [
        pltpu.make_async_copy(docs_hbm, docs_ref, in_sem.at[0]),
        pltpu.make_async_copy(win_hbm, win_ref, in_sem.at[1]),
        pltpu.make_async_copy(q_hbm, q_ref, in_sem.at[2]),
    ]
    for cp in loads:
        cp.start()

    barrier = pltpu.get_barrier_semaphore()

    def greet(peer):
        pl.semaphore_signal(barrier, inc=1, device_id=peer, device_id_type=MESH)

    greet(sib)
    greet(cross)

    @pl.when(jnp.logical_not(last))
    def _():
        greet(succ)

    @pl.when(jnp.logical_not(first))
    def _():
        greet(pred)

    @pl.when(first)
    def _():
        greet(first_next)
        greet(first_prev)
        greet(last_here)

    @pl.when(last)
    def _():
        greet(last_next)
        greet(last_prev)
        greet(first_here)

    pl.semaphore_wait(barrier, 4 + 2 * first.astype(jnp.int32) + 2 * last.astype(jnp.int32))

    owns = [pltpu.make_async_copy(inputs[p], at(p, 0, q), own_sem.at[p]) for p in range(2)]
    for cp in owns:
        cp.start()

    def remote(p, src, k, col, peer, sem):
        return pltpu.make_async_remote_copy(
            src_ref=src,
            dst_ref=at(p, k, col),
            send_sem=sem.at[p],
            recv_sem=recv_sem.at[p, k, col],
            device_id=peer,
            device_id_type=MESH,
        )

    def hop_at(p, k):
        return hops[p].at[pl.ds(k * BLK, BLK)]

    def to_hop(p, src, k, peer):
        return pltpu.make_async_remote_copy(
            src_ref=src,
            dst_ref=hop_at(p, k),
            send_sem=relay_sem.at[k, p],
            recv_sem=hop_sem.at[p, k],
            device_id=peer,
            device_id_type=MESH,
        )

    def onward(p, k, peer):
        return pltpu.make_async_remote_copy(
            src_ref=hop_at(p, k),
            dst_ref=at(p, k + 1, q),
            send_sem=onward_sem.at[k, p],
            recv_sem=recv_sem.at[p, k + 1, q],
            device_id=peer,
            device_id_type=MESH,
        )

    def pass_on(k, peer):
        for p in range(2):
            to_hop(p, hop_at(p, k), k, peer).wait_recv()
        for p in range(2):
            onward(p, k, peer).start()

    def source(p, k, col):
        return inputs[p] if k == 0 else at(p, k, col)

    sends = []
    for k in range(DEPTH):
        if k % 2 == 1 and k + 1 < DEPTH:
            pl.when(first)(functools.partial(pass_on, k, first_next))
        if k > 0:
            for p in range(2):
                remote(p, source(p, k, q), k, q, pred, relay_sem.at[k - 1]).wait_recv()
        if k + 1 < DEPTH:
            via = last_next if k % 2 == 0 else first_here

            @pl.when(jnp.logical_not(last))
            def _():
                for p in range(2):
                    remote(p, source(p, k, q), k + 1, q, succ, relay_sem.at[k]).start()

            @pl.when(last)
            def _():
                for p in range(2):
                    to_hop(p, source(p, k, q), k, via).start()

            if k % 2 == 0:
                pl.when(last)(functools.partial(pass_on, k, first_here))
        for p in range(2):
            cp = remote(p, source(p, k, q), k, q, cross, cross_sem.at[k])
            cp.start()
            sends.append(cp)
        for p in range(2):
            cp = remote(p, source(p, k, q), k, q, sib, sib_sem.at[k])
            cp.start()
            sends.append(cp)
        if k == 0:
            loads[0].wait()
            loads[1].wait()
            head = lax.broadcasted_iota(jnp.int32, (heads, BLK), 0)
            win8 = jnp.zeros((heads, BLK), jnp.int32)
            for h in range(heads):
                win8 = jnp.where(head == h, win_ref[h], win8)
            doc_here = docs_ref[g]
            for slot in range(DEPTH * LEVEL):
                d = LEVEL * (slot // LEVEL) + q - slot % LEVEL
                kb = g - d
                doc_there = docs_ref[(kb + n_blocks) % n_blocks]
                live = (d >= 0) & (d < WMAX) & (kb >= 0) & (doc_there == doc_here)
                keep = (win8 > d) & (jnp.full((heads, BLK), live.astype(jnp.int32)) > 0)
                bias_sc[:, pl.ds(slot * BLK, BLK)] = jnp.where(keep, 0.0, -jnp.inf).astype(jnp.float32)

    for k in range(DEPTH):
        for p in range(2):
            got_cross = at(p, k, cross_q)
            remote(p, got_cross, k, cross_q, cross, cross_sem.at[k]).wait_recv()
            cp = remote(p, got_cross, k, cross_q, sib, fwd_sem.at[k])
            cp.start()
            sends.append(cp)

    for k in range(DEPTH):
        for p in range(2):
            remote(p, at(p, k, sib_q), k, sib_q, sib, sib_sem.at[k]).wait_recv()
        for p in range(2):
            remote(p, at(p, k, far_q), k, far_q, sib, fwd_sem.at[k]).wait_recv()
    for cp in owns:
        cp.wait()
    loads[2].wait()

    scale = hd ** -0.5
    own = pl.multiple_of(q * BLK, BLK)
    ones = jnp.ones((keys, BLK), jnp.bfloat16)

    def one_chunk(ci, carry):
        r0 = pl.multiple_of(ci * chunk, chunk)
        qc = q_ref[pl.ds(r0, chunk), :]
        sc = lax.dot_general(qc, got_k[...], (((1,), (1,)), ((), ())), preferred_element_type=jnp.float32) * scale
        sc = (sc.reshape(chunk // heads, heads, keys) + bias_sc[...][None]).reshape(chunk, keys)
        s_sc[...] = sc
        query_i = (lax.broadcasted_iota(jnp.int32, (chunk, BLK), 0) + r0) // heads
        key_j = lax.broadcasted_iota(jnp.int32, (chunk, BLK), 1)
        s_sc[:, pl.ds(own, BLK)] = jnp.where(key_j <= query_i, s_sc[:, pl.ds(own, BLK)], -jnp.inf)
        sc = s_sc[...]
        m = jnp.max(sc, axis=1, keepdims=True)
        w = jnp.exp(sc - m).astype(jnp.bfloat16)
        num = jnp.dot(w, got_v[...], preferred_element_type=jnp.float32)
        den = jnp.dot(w, ones, preferred_element_type=jnp.float32)
        out_ref[pl.ds(r0, chunk), :] = (num / den[:, :1]).astype(out_ref.dtype)
        return carry

    lax.fori_loop(0, rows // chunk, one_chunk, 0)

    for cp in sends:
        cp.wait_send()
    for k in range(DEPTH - 1):
        for p in range(2):
            remote(p, at(p, k, q), k + 1, q, succ, relay_sem.at[k]).wait_send()
        if k % 2 == 0:
            role = last
            peer = first_here
        else:
            role = first
            peer = first_next

        @pl.when(role)
        def _():
            for p in range(2):
                onward(p, k, peer).wait_send()


def fused(block_docs, windows, key_rows, value_rows, q2, n_ctx, n_sub):
    rows, hd = q2.shape
    keys = DEPTH * LEVEL * BLK
    chunk = 256
    heads = windows.shape[0]
    return pl.pallas_call(
        functools.partial(fused_kernel, n_ctx, n_sub),
        out_shape=jax.ShapeDtypeStruct((rows, hd), q2.dtype),
        in_specs=[pl.BlockSpec(memory_space=pltpu.HBM)] * 5,
        out_specs=pl.BlockSpec(memory_space=pltpu.VMEM),
        scratch_shapes=[
            pltpu.VMEM((keys, hd), key_rows.dtype),
            pltpu.VMEM((keys, hd), value_rows.dtype),
            pltpu.VMEM((heads, keys), jnp.float32),
            pltpu.VMEM((chunk, keys), jnp.float32),
            pltpu.VMEM((rows, hd), q2.dtype),
            pltpu.SMEM(block_docs.shape, jnp.int32),
            pltpu.SMEM(windows.shape, jnp.int32),
            pltpu.SemaphoreType.DMA((3,)),
            pltpu.SemaphoreType.DMA((2, DEPTH, LEVEL)),
            pltpu.SemaphoreType.DMA((DEPTH, 2)),
            pltpu.SemaphoreType.DMA((DEPTH, 2)),
            pltpu.SemaphoreType.DMA((DEPTH, 2)),
            pltpu.SemaphoreType.DMA((DEPTH, 2)),
            pltpu.SemaphoreType.DMA((2,)),
            pltpu.VMEM(((DEPTH - 1) * BLK, hd), key_rows.dtype),
            pltpu.VMEM(((DEPTH - 1) * BLK, hd), value_rows.dtype),
            pltpu.SemaphoreType.DMA((2, DEPTH - 1)),
            pltpu.SemaphoreType.DMA((DEPTH - 1, 2)),
        ],
        compiler_params=pltpu.CompilerParams(
            collective_id=0, has_side_effects=True, vmem_limit_bytes=67043328
        ),
    )(block_docs, windows, key_rows, value_rows, q2)


def local(queries, key_rows, value_rows, block_docs, windows):
    n_ctx = lax.axis_size("ctx")
    n_sub = lax.axis_size("sub")
    rows_here, heads, hd = queries.shape
    out = fused(block_docs, windows, key_rows, value_rows, queries.reshape(rows_here * heads, hd), n_ctx, n_sub)
    return out.reshape(rows_here, heads, hd)


def solution(mesh):
    in_specs = (
        P(("ctx", "sub"), None, None),
        P(("ctx", "sub"), None),
        P(("ctx", "sub"), None),
        P(),
        P(),
    )
    out_specs = P(("ctx", "sub"), None, None)
    return jax.shard_map(local, mesh=mesh, in_specs=in_specs, out_specs=out_specs, check_vma=False)
```

```python
import functools

import jax
import jax.numpy as jnp
from jax import lax
from jax.experimental import pallas as pl
from jax.experimental.pallas import tpu as pltpu
from jax.sharding import PartitionSpec as P

BLK = 128
WMAX = 32
LEVEL = 4
DEPTH = (WMAX - 1 + LEVEL - 1) // LEVEL + 1
MESH = pl.DeviceIdType.MESH


def fused_kernel(n_ctx, n_sub, docs_hbm, win_hbm, k_ref, v_ref, q_hbm, out_ref,
                 got_kv, bias_sc, s_sc, q_ref, docs_ref, win_ref, in_sem,
                 recv_sem, relay_sem, sib_sem, cross_sem, fwd_sem, own_sem):
    c = lax.axis_index("ctx")
    s = lax.axis_index("sub")
    total = n_ctx * n_sub
    g = c * n_sub + s
    q = s % LEVEL
    succ_g = (g + LEVEL) % total
    pred_g = (g + total - LEVEL) % total
    succ = (succ_g // n_sub, succ_g % n_sub)
    pred = (pred_g // n_sub, pred_g % n_sub)
    sib_q = q + 1 - 2 * (q % 2)
    cross_q = q + 2 - 4 * ((q // 2) % 2)
    far_q = 3 - q
    sib = (c, s - q + sib_q)
    cross = (c, s - q + cross_q)
    got_k = got_kv.at[0]
    got_v = got_kv.at[1]
    planes = (got_k, got_v)
    inputs = (k_ref, v_ref)
    rows, hd = q_ref.shape
    chunk, keys = s_sc.shape
    heads = bias_sc.shape[0]
    n_blocks = docs_ref.shape[0]

    def at(p, k, col):
        return planes[p].at[pl.ds(pl.multiple_of((k * LEVEL + col) * BLK, BLK), BLK)]

    def both(k, col):
        return got_kv.at[:, pl.ds(pl.multiple_of((k * LEVEL + col) * BLK, BLK), BLK)]

    loads = [
        pltpu.make_async_copy(docs_hbm, docs_ref, in_sem.at[0]),
        pltpu.make_async_copy(win_hbm, win_ref, in_sem.at[1]),
        pltpu.make_async_copy(q_hbm, q_ref, in_sem.at[2]),
    ]
    for cp in loads:
        cp.start()

    barrier = pltpu.get_barrier_semaphore()
    for peer in (succ, pred, sib, cross):
        pl.semaphore_signal(barrier, inc=1, device_id=peer, device_id_type=MESH)
    pl.semaphore_wait(barrier, 4)

    owns = [pltpu.make_async_copy(inputs[p], at(p, 0, q), own_sem.at[p]) for p in range(2)]
    for cp in owns:
        cp.start()

    def remote(p, src, k, col, peer, sem):
        return pltpu.make_async_remote_copy(
            src_ref=src,
            dst_ref=at(p, k, col),
            send_sem=sem.at[p],
            recv_sem=recv_sem.at[p, k, col],
            device_id=peer,
            device_id_type=MESH,
        )

    def block(src_k, src_col, k, col, peer, sem):
        return pltpu.make_async_remote_copy(
            src_ref=both(src_k, src_col),
            dst_ref=both(k, col),
            send_sem=sem.at[0],
            recv_sem=recv_sem.at[0, k, col],
            device_id=peer,
            device_id_type=MESH,
        )

    def send(k_src, col_src, k, col, peer, sem, out):
        if k_src == 0 and col_src is q:
            for p in range(2):
                cp = remote(p, inputs[p], k, col, peer, sem)
                cp.start()
                out.append(cp)
        else:
            cp = block(k_src, col_src, k, col, peer, sem)
            cp.start()
            out.append(cp)

    def arrive(k, col, peer, sem):
        if k == 0 and col is q:
            raise ValueError("own slot")
        block(k, col, k, col, peer, sem).wait_recv()

    def arrive_own_from(k, col, peer, sem, single):
        if single:
            for p in range(2):
                remote(p, at(p, k, col), k, col, peer, sem).wait_recv()
        else:
            block(k, col, k, col, peer, sem).wait_recv()

    def source(p, k, col):
        return inputs[p] if k == 0 else at(p, k, col)

    sends = []
    for k in range(DEPTH):
        if k > 0:
            arrive_own_from(k, q, pred, relay_sem.at[k - 1], k == 1)
        if k + 1 < DEPTH:
            send(k, q, k + 1, q, succ, relay_sem.at[k], sends)
        send(k, q, k, q, cross, cross_sem.at[k], sends)
        send(k, q, k, q, sib, sib_sem.at[k], sends)
        if k == 0:
            loads[0].wait()
            loads[1].wait()
            head = lax.broadcasted_iota(jnp.int32, (heads, BLK), 0)
            win8 = jnp.zeros((heads, BLK), jnp.int32)
            for h in range(heads):
                win8 = jnp.where(head == h, win_ref[h], win8)
            doc_here = docs_ref[g]
            for slot in range(DEPTH * LEVEL):
                d = LEVEL * (slot // LEVEL) + q - slot % LEVEL
                kb = g - d
                doc_there = docs_ref[(kb + n_blocks) % n_blocks]
                live = (d >= 0) & (d < WMAX) & (kb >= 0) & (doc_there == doc_here)
                keep = (win8 > d) & (jnp.full((heads, BLK), live.astype(jnp.int32)) > 0)
                bias_sc[:, pl.ds(slot * BLK, BLK)] = jnp.where(keep, 0.0, -jnp.inf).astype(jnp.float32)

    for k in range(DEPTH):
        arrive_own_from(k, cross_q, cross, cross_sem.at[k], k == 0)
        send(k, cross_q, k, cross_q, sib, fwd_sem.at[k], sends)

    for k in range(DEPTH):
        arrive_own_from(k, sib_q, sib, sib_sem.at[k], k == 0)
        arrive(k, far_q, sib, fwd_sem.at[k])
    for cp in owns:
        cp.wait()
    loads[2].wait()

    scale = hd ** -0.5
    own = pl.multiple_of(q * BLK, BLK)
    ones = jnp.ones((keys, BLK), jnp.bfloat16)

    def one_chunk(ci, carry):
        r0 = pl.multiple_of(ci * chunk, chunk)
        qc = q_ref[pl.ds(r0, chunk), :]
        sc = lax.dot_general(qc, got_k[...], (((1,), (1,)), ((), ())), preferred_element_type=jnp.float32) * scale
        sc = (sc.reshape(chunk // heads, heads, keys) + bias_sc[...][None]).reshape(chunk, keys)
        s_sc[...] = sc
        query_i = (lax.broadcasted_iota(jnp.int32, (chunk, BLK), 0) + r0) // heads
        key_j = lax.broadcasted_iota(jnp.int32, (chunk, BLK), 1)
        s_sc[:, pl.ds(own, BLK)] = jnp.where(key_j <= query_i, s_sc[:, pl.ds(own, BLK)], -jnp.inf)
        sc = s_sc[...]
        m = jnp.max(sc, axis=1, keepdims=True)
        w = jnp.exp(sc - m).astype(jnp.bfloat16)
        num = jnp.dot(w, got_v[...], preferred_element_type=jnp.float32)
        den = jnp.dot(w, ones, preferred_element_type=jnp.float32)
        out_ref[pl.ds(r0, chunk), :] = (num / den[:, :1]).astype(out_ref.dtype)
        return carry

    lax.fori_loop(0, rows // chunk, one_chunk, 0)

    for cp in sends:
        cp.wait_send()


def fused(block_docs, windows, key_rows, value_rows, q2, n_ctx, n_sub):
    rows, hd = q2.shape
    keys = DEPTH * LEVEL * BLK
    chunk = 256
    heads = windows.shape[0]
    return pl.pallas_call(
        functools.partial(fused_kernel, n_ctx, n_sub),
        out_shape=jax.ShapeDtypeStruct((rows, hd), q2.dtype),
        in_specs=[pl.BlockSpec(memory_space=pltpu.HBM)] * 5,
        out_specs=pl.BlockSpec(memory_space=pltpu.VMEM),
        scratch_shapes=[
            pltpu.VMEM((2, keys, hd), key_rows.dtype),
            pltpu.VMEM((heads, keys), jnp.float32),
            pltpu.VMEM((chunk, keys), jnp.float32),
            pltpu.VMEM((rows, hd), q2.dtype),
            pltpu.SMEM(block_docs.shape, jnp.int32),
            pltpu.SMEM(windows.shape, jnp.int32),
            pltpu.SemaphoreType.DMA((3,)),
            pltpu.SemaphoreType.DMA((2, DEPTH, LEVEL)),
            pltpu.SemaphoreType.DMA((DEPTH, 2)),
            pltpu.SemaphoreType.DMA((DEPTH, 2)),
            pltpu.SemaphoreType.DMA((DEPTH, 2)),
            pltpu.SemaphoreType.DMA((DEPTH, 2)),
            pltpu.SemaphoreType.DMA((2,)),
        ],
        compiler_params=pltpu.CompilerParams(
            collective_id=0, has_side_effects=True, vmem_limit_bytes=67043328
        ),
    )(block_docs, windows, key_rows, value_rows, q2)


def local(queries, key_rows, value_rows, block_docs, windows):
    n_ctx = lax.axis_size("ctx")
    n_sub = lax.axis_size("sub")
    rows_here, heads, hd = queries.shape
    out = fused(block_docs, windows, key_rows, value_rows, queries.reshape(rows_here * heads, hd), n_ctx, n_sub)
    return out.reshape(rows_here, heads, hd)


def solution(mesh):
    in_specs = (
        P(("ctx", "sub"), None, None),
        P(("ctx", "sub"), None),
        P(("ctx", "sub"), None),
        P(),
        P(),
    )
    out_specs = P(("ctx", "sub"), None, None)
    return jax.shard_map(local, mesh=mesh, in_specs=in_specs, out_specs=out_specs, check_vma=False)
```

```python
import functools

import jax
import jax.numpy as jnp
from jax import lax
from jax.experimental import pallas as pl
from jax.experimental.pallas import tpu as pltpu
from jax.sharding import PartitionSpec as P

BLK = 128
WMAX = 32
LEVEL = 4
DEPTH = (WMAX - 1 + LEVEL - 1) // LEVEL + 1
MESH = pl.DeviceIdType.MESH


def fused_kernel(n_ctx, n_sub, docs_hbm, win_hbm, k_ref, v_ref, q_hbm, out_ref,
                 got_k, got_v, bias_sc, s_sc, q_ref, docs_ref, win_ref, in_sem,
                 recv_sem, relay_sem, sib_sem, cross_sem, fwd_sem, own_sem):
    c = lax.axis_index("ctx")
    s = lax.axis_index("sub")
    total = n_ctx * n_sub
    g = c * n_sub + s
    q = s % LEVEL
    succ_g = (g + LEVEL) % total
    pred_g = (g + total - LEVEL) % total
    succ = (succ_g // n_sub, succ_g % n_sub)
    pred = (pred_g // n_sub, pred_g % n_sub)
    sib_q = q + 1 - 2 * (q % 2)
    cross_q = q + 2 - 4 * ((q // 2) % 2)
    far_q = 3 - q
    sib = (c, s - q + sib_q)
    cross = (c, s - q + cross_q)
    planes = (got_k, got_v)
    inputs = (k_ref, v_ref)
    rows, hd = q_ref.shape
    chunk, keys = s_sc.shape
    heads = bias_sc.shape[0]
    n_blocks = docs_ref.shape[0]

    def at(p, k, col):
        return planes[p].at[pl.ds(pl.multiple_of((k * LEVEL + col) * BLK, BLK), BLK)]

    loads = [
        pltpu.make_async_copy(docs_hbm, docs_ref, in_sem.at[0]),
        pltpu.make_async_copy(win_hbm, win_ref, in_sem.at[1]),
        pltpu.make_async_copy(q_hbm, q_ref, in_sem.at[2]),
    ]
    for cp in loads:
        cp.start()

    barrier = pltpu.get_barrier_semaphore()
    for peer in (succ, pred, sib, cross):
        pl.semaphore_signal(barrier, inc=1, device_id=peer, device_id_type=MESH)
    pl.semaphore_wait(barrier, 4)

    owns = [pltpu.make_async_copy(inputs[p], at(p, 0, q), own_sem.at[p]) for p in range(2)]
    for cp in owns:
        cp.start()

    def remote(p, src, k, col, peer, sem):
        return pltpu.make_async_remote_copy(
            src_ref=src,
            dst_ref=at(p, k, col),
            send_sem=sem.at[p],
            recv_sem=recv_sem.at[p, k, col],
            device_id=peer,
            device_id_type=MESH,
        )

    def source(p, k, col):
        return inputs[p] if k == 0 else at(p, k, col)

    sends = []
    for k in range(DEPTH):
        if k > 0:
            for p in range(2):
                remote(p, source(p, k, q), k, q, pred, relay_sem.at[k - 1]).wait_recv()
        if k + 1 < DEPTH:
            for p in range(2):
                cp = remote(p, source(p, k, q), k + 1, q, succ, relay_sem.at[k])
                cp.start()
                sends.append(cp)
        for p in range(2):
            cp = remote(p, source(p, k, q), k, q, cross, cross_sem.at[k])
            cp.start()
            sends.append(cp)
        for p in range(2):
            cp = remote(p, source(p, k, q), k, q, sib, sib_sem.at[k])
            cp.start()
            sends.append(cp)
        if k == 0:
            loads[0].wait()
            loads[1].wait()
            head = lax.broadcasted_iota(jnp.int32, (heads, BLK), 0)
            win8 = jnp.zeros((heads, BLK), jnp.int32)
            for h in range(heads):
                win8 = jnp.where(head == h, win_ref[h], win8)
            doc_here = docs_ref[g]
            for slot in range(DEPTH * LEVEL):
                d = LEVEL * (slot // LEVEL) + q - slot % LEVEL
                kb = g - d
                doc_there = docs_ref[(kb + n_blocks) % n_blocks]
                live = (d >= 0) & (d < WMAX) & (kb >= 0) & (doc_there == doc_here)
                keep = (win8 > d) & (jnp.full((heads, BLK), live.astype(jnp.int32)) > 0)
                bias_sc[:, pl.ds(slot * BLK, BLK)] = jnp.where(keep, 0.0, -jnp.inf).astype(jnp.float32)

    for k in range(DEPTH):
        for p in range(2):
            got_cross = at(p, k, cross_q)
            remote(p, got_cross, k, cross_q, cross, cross_sem.at[k]).wait_recv()
            cp = remote(p, got_cross, k, cross_q, sib, fwd_sem.at[k])
            cp.start()
            sends.append(cp)

    for k in range(DEPTH):
        for p in range(2):
            remote(p, at(p, k, sib_q), k, sib_q, sib, sib_sem.at[k]).wait_recv()
        for p in range(2):
            remote(p, at(p, k, far_q), k, far_q, sib, fwd_sem.at[k]).wait_recv()
    for cp in owns:
        cp.wait()
    loads[2].wait()

    scale = hd ** -0.5
    own = pl.multiple_of(q * BLK, BLK)
    ones = jnp.ones((keys, BLK), jnp.bfloat16)

    def one_chunk(ci, carry):
        r0 = pl.multiple_of(ci * chunk, chunk)
        qc = q_ref[pl.ds(r0, chunk), :]
        sc = lax.dot_general(qc, got_k[...], (((1,), (1,)), ((), ())), preferred_element_type=jnp.float32) * scale
        sc = (sc.reshape(chunk // heads, heads, keys) + bias_sc[...][None]).reshape(chunk, keys)
        s_sc[...] = sc
        query_i = (lax.broadcasted_iota(jnp.int32, (chunk, BLK), 0) + r0) // heads
        key_j = lax.broadcasted_iota(jnp.int32, (chunk, BLK), 1)
        s_sc[:, pl.ds(own, BLK)] = jnp.where(key_j <= query_i, s_sc[:, pl.ds(own, BLK)], -jnp.inf)
        sc = s_sc[...]
        m = jnp.max(sc, axis=1, keepdims=True)
        w = jnp.exp(sc - m).astype(jnp.bfloat16)
        num = jnp.dot(w, got_v[...], preferred_element_type=jnp.float32)
        den = jnp.dot(w, ones, preferred_element_type=jnp.float32)
        out_ref[pl.ds(r0, chunk), :] = (num / den[:, :1]).astype(out_ref.dtype)
        return carry

    lax.fori_loop(0, rows // chunk, one_chunk, 0)

    for cp in sends:
        cp.wait_send()


def fused(block_docs, windows, key_rows, value_rows, q2, n_ctx, n_sub):
    rows, hd = q2.shape
    keys = DEPTH * LEVEL * BLK
    chunk = 512
    heads = windows.shape[0]
    return pl.pallas_call(
        functools.partial(fused_kernel, n_ctx, n_sub),
        out_shape=jax.ShapeDtypeStruct((rows, hd), q2.dtype),
        in_specs=[pl.BlockSpec(memory_space=pltpu.HBM)] * 5,
        out_specs=pl.BlockSpec(memory_space=pltpu.VMEM),
        scratch_shapes=[
            pltpu.VMEM((keys, hd), key_rows.dtype),
            pltpu.VMEM((keys, hd), value_rows.dtype),
            pltpu.VMEM((heads, keys), jnp.float32),
            pltpu.VMEM((chunk, keys), jnp.float32),
            pltpu.VMEM((rows, hd), q2.dtype),
            pltpu.SMEM(block_docs.shape, jnp.int32),
            pltpu.SMEM(windows.shape, jnp.int32),
            pltpu.SemaphoreType.DMA((3,)),
            pltpu.SemaphoreType.DMA((2, DEPTH, LEVEL)),
            pltpu.SemaphoreType.DMA((DEPTH, 2)),
            pltpu.SemaphoreType.DMA((DEPTH, 2)),
            pltpu.SemaphoreType.DMA((DEPTH, 2)),
            pltpu.SemaphoreType.DMA((DEPTH, 2)),
            pltpu.SemaphoreType.DMA((2,)),
        ],
        compiler_params=pltpu.CompilerParams(
            collective_id=0, has_side_effects=True, vmem_limit_bytes=67043328
        ),
    )(block_docs, windows, key_rows, value_rows, q2)


def local(queries, key_rows, value_rows, block_docs, windows):
    n_ctx = lax.axis_size("ctx")
    n_sub = lax.axis_size("sub")
    rows_here, heads, hd = queries.shape
    out = fused(block_docs, windows, key_rows, value_rows, queries.reshape(rows_here * heads, hd), n_ctx, n_sub)
    return out.reshape(rows_here, heads, hd)


def solution(mesh):
    in_specs = (
        P(("ctx", "sub"), None, None),
        P(("ctx", "sub"), None),
        P(("ctx", "sub"), None),
        P(),
        P(),
    )
    out_specs = P(("ctx", "sub"), None, None)
    return jax.shard_map(local, mesh=mesh, in_specs=in_specs, out_specs=out_specs, check_vma=False)
```

```python
import functools

import jax
import jax.numpy as jnp
from jax import lax
from jax.experimental import pallas as pl
from jax.experimental.pallas import tpu as pltpu
from jax.sharding import PartitionSpec as P

BLK = 128
WMAX = 32
LEVEL = 4
DEPTH = (WMAX - 1 + LEVEL - 1) // LEVEL + 1
MESH = pl.DeviceIdType.MESH


def fused_kernel(n_ctx, n_sub, docs_hbm, win_hbm, k_ref, v_ref, q_hbm, out_ref,
                 got_k, got_v, bias_sc, s_sc, q_ref, docs_ref, win_ref, in_sem,
                 recv_sem, relay_sem, sib_sem, cross_sem, fwd_sem, own_sem):
    c = lax.axis_index("ctx")
    s = lax.axis_index("sub")
    total = n_ctx * n_sub
    g = c * n_sub + s
    q = s % LEVEL
    succ_g = (g + LEVEL) % total
    pred_g = (g + total - LEVEL) % total
    succ = (succ_g // n_sub, succ_g % n_sub)
    pred = (pred_g // n_sub, pred_g % n_sub)
    sib_q = q + 1 - 2 * (q % 2)
    cross_q = q + 2 - 4 * ((q // 2) % 2)
    far_q = 3 - q
    sib = (c, s - q + sib_q)
    cross = (c, s - q + cross_q)
    planes = (got_k, got_v)
    inputs = (k_ref, v_ref)
    rows, hd = q_ref.shape
    chunk, keys = s_sc.shape
    heads = bias_sc.shape[0]
    n_blocks = docs_ref.shape[0]

    def at(p, k, col):
        return planes[p].at[pl.ds(pl.multiple_of((k * LEVEL + col) * BLK, BLK), BLK)]

    loads = [
        pltpu.make_async_copy(docs_hbm, docs_ref, in_sem.at[0]),
        pltpu.make_async_copy(win_hbm, win_ref, in_sem.at[1]),
        pltpu.make_async_copy(q_hbm, q_ref, in_sem.at[2]),
    ]
    for cp in loads:
        cp.start()

    barrier = pltpu.get_barrier_semaphore()
    for peer in (succ, pred, sib, cross):
        pl.semaphore_signal(barrier, inc=1, device_id=peer, device_id_type=MESH)
    pl.semaphore_wait(barrier, 4)

    owns = [pltpu.make_async_copy(inputs[p], at(p, 0, q), own_sem.at[p]) for p in range(2)]
    for cp in owns:
        cp.start()

    def remote(p, src, k, col, peer, sem):
        return pltpu.make_async_remote_copy(
            src_ref=src,
            dst_ref=at(p, k, col),
            send_sem=sem.at[p],
            recv_sem=recv_sem.at[p, k, col],
            device_id=peer,
            device_id_type=MESH,
        )

    def source(p, k, col):
        return inputs[p] if k == 0 else at(p, k, col)

    sends = []
    for k in range(DEPTH):
        if k > 0:
            for p in range(2):
                remote(p, source(p, k, q), k, q, pred, relay_sem.at[k - 1]).wait_recv()
        if k + 1 < DEPTH:
            for p in range(2):
                cp = remote(p, source(p, k, q), k + 1, q, succ, relay_sem.at[k])
                cp.start()
                sends.append(cp)
        for p in range(2):
            cp = remote(p, source(p, k, q), k, q, cross, cross_sem.at[k])
            cp.start()
            sends.append(cp)
        for p in range(2):
            cp = remote(p, source(p, k, q), k, q, sib, sib_sem.at[k])
            cp.start()
            sends.append(cp)
        if k == 0:
            loads[0].wait()
            loads[1].wait()
            head = lax.broadcasted_iota(jnp.int32, (heads, BLK), 0)
            win8 = jnp.zeros((heads, BLK), jnp.int32)
            for h in range(heads):
                win8 = jnp.where(head == h, win_ref[h], win8)
            doc_here = docs_ref[g]
            for slot in range(DEPTH * LEVEL):
                d = LEVEL * (slot // LEVEL) + q - slot % LEVEL
                kb = g - d
                doc_there = docs_ref[(kb + n_blocks) % n_blocks]
                live = (d >= 0) & (d < WMAX) & (kb >= 0) & (doc_there == doc_here)
                keep = (win8 > d) & (jnp.full((heads, BLK), live.astype(jnp.int32)) > 0)
                bias_sc[:, pl.ds(slot * BLK, BLK)] = jnp.where(keep, 0.0, -jnp.inf).astype(jnp.float32)

    for k in range(DEPTH):
        for p in range(2):
            got_cross = at(p, k, cross_q)
            remote(p, got_cross, k, cross_q, cross, cross_sem.at[k]).wait_recv()
            cp = remote(p, got_cross, k, cross_q, sib, fwd_sem.at[k])
            cp.start()
            sends.append(cp)

    for k in range(DEPTH):
        for p in range(2):
            remote(p, at(p, k, sib_q), k, sib_q, sib, sib_sem.at[k]).wait_recv()
        for p in range(2):
            remote(p, at(p, k, far_q), k, far_q, sib, fwd_sem.at[k]).wait_recv()
    for cp in owns:
        cp.wait()
    loads[2].wait()

    scale = hd ** -0.5
    own = pl.multiple_of(q * BLK, BLK)
    ones = jnp.ones((keys, BLK), jnp.bfloat16)

    def one_chunk(ci, carry):
        r0 = pl.multiple_of(ci * chunk, chunk)
        qc = q_ref[pl.ds(r0, chunk), :]
        sc = lax.dot_general(qc, got_k[...], (((1,), (1,)), ((), ())), preferred_element_type=jnp.float32) * scale
        sc = (sc.reshape(chunk // heads, heads, keys) + bias_sc[...][None]).reshape(chunk, keys)
        s_sc[...] = sc
        query_i = (lax.broadcasted_iota(jnp.int32, (chunk, BLK), 0) + r0) // heads
        key_j = lax.broadcasted_iota(jnp.int32, (chunk, BLK), 1)
        s_sc[:, pl.ds(own, BLK)] = jnp.where(key_j <= query_i, s_sc[:, pl.ds(own, BLK)], -jnp.inf)
        sc = s_sc[...]
        m = jnp.max(sc, axis=1, keepdims=True)
        w = jnp.exp(sc - m).astype(jnp.bfloat16)
        num = jnp.dot(w, got_v[...], preferred_element_type=jnp.float32)
        den = jnp.dot(w, ones, preferred_element_type=jnp.float32)
        out_ref[pl.ds(r0, chunk), :] = (num / den[:, :1]).astype(out_ref.dtype)
        return carry

    lax.fori_loop(0, rows // chunk, one_chunk, 0)

    for cp in sends:
        cp.wait_send()


def fused(block_docs, windows, key_rows, value_rows, q2, n_ctx, n_sub):
    rows, hd = q2.shape
    keys = DEPTH * LEVEL * BLK
    chunk = 1024
    heads = windows.shape[0]
    return pl.pallas_call(
        functools.partial(fused_kernel, n_ctx, n_sub),
        out_shape=jax.ShapeDtypeStruct((rows, hd), q2.dtype),
        in_specs=[pl.BlockSpec(memory_space=pltpu.HBM)] * 5,
        out_specs=pl.BlockSpec(memory_space=pltpu.VMEM),
        scratch_shapes=[
            pltpu.VMEM((keys, hd), key_rows.dtype),
            pltpu.VMEM((keys, hd), value_rows.dtype),
            pltpu.VMEM((heads, keys), jnp.float32),
            pltpu.VMEM((chunk, keys), jnp.float32),
            pltpu.VMEM((rows, hd), q2.dtype),
            pltpu.SMEM(block_docs.shape, jnp.int32),
            pltpu.SMEM(windows.shape, jnp.int32),
            pltpu.SemaphoreType.DMA((3,)),
            pltpu.SemaphoreType.DMA((2, DEPTH, LEVEL)),
            pltpu.SemaphoreType.DMA((DEPTH, 2)),
            pltpu.SemaphoreType.DMA((DEPTH, 2)),
            pltpu.SemaphoreType.DMA((DEPTH, 2)),
            pltpu.SemaphoreType.DMA((DEPTH, 2)),
            pltpu.SemaphoreType.DMA((2,)),
        ],
        compiler_params=pltpu.CompilerParams(
            collective_id=0, has_side_effects=True, vmem_limit_bytes=67043328
        ),
    )(block_docs, windows, key_rows, value_rows, q2)


def local(queries, key_rows, value_rows, block_docs, windows):
    n_ctx = lax.axis_size("ctx")
    n_sub = lax.axis_size("sub")
    rows_here, heads, hd = queries.shape
    out = fused(block_docs, windows, key_rows, value_rows, queries.reshape(rows_here * heads, hd), n_ctx, n_sub)
    return out.reshape(rows_here, heads, hd)


def solution(mesh):
    in_specs = (
        P(("ctx", "sub"), None, None),
        P(("ctx", "sub"), None),
        P(("ctx", "sub"), None),
        P(),
        P(),
    )
    out_specs = P(("ctx", "sub"), None, None)
    return jax.shard_map(local, mesh=mesh, in_specs=in_specs, out_specs=out_specs, check_vma=False)
```

```python
import functools

import jax
import jax.numpy as jnp
from jax import lax
from jax.experimental import pallas as pl
from jax.experimental.pallas import tpu as pltpu
from jax.sharding import PartitionSpec as P

BLK = 128
WMAX = 32
LEVEL = 4
DEPTH = (WMAX - 1 + LEVEL - 1) // LEVEL + 1
MESH = pl.DeviceIdType.MESH


def fused_kernel(n_ctx, n_sub, docs_hbm, win_hbm, k_ref, v_ref, q_hbm, out_ref,
                 got_k, got_v, bias_sc, s_sc, q_ref, docs_ref, win_ref, in_sem,
                 recv_sem, relay_sem, sib_sem, cross_sem, fwd_sem, own_sem):
    c = lax.axis_index("ctx")
    s = lax.axis_index("sub")
    total = n_ctx * n_sub
    g = c * n_sub + s
    q = s % LEVEL
    succ_g = (g + LEVEL) % total
    pred_g = (g + total - LEVEL) % total
    succ = (succ_g // n_sub, succ_g % n_sub)
    pred = (pred_g // n_sub, pred_g % n_sub)
    sib_q = q + 1 - 2 * (q % 2)
    cross_q = q + 2 - 4 * ((q // 2) % 2)
    far_q = 3 - q
    sib = (c, s - q + sib_q)
    cross = (c, s - q + cross_q)
    planes = (got_k, got_v)
    inputs = (k_ref, v_ref)
    rows, hd = q_ref.shape
    chunk, keys = s_sc.shape
    heads = bias_sc.shape[0]
    n_blocks = docs_ref.shape[0]

    def at(p, k, col):
        return planes[p].at[pl.ds(pl.multiple_of((k * LEVEL + col) * BLK, BLK), BLK)]

    loads = [
        pltpu.make_async_copy(docs_hbm, docs_ref, in_sem.at[0]),
        pltpu.make_async_copy(win_hbm, win_ref, in_sem.at[1]),
        pltpu.make_async_copy(q_hbm, q_ref, in_sem.at[2]),
    ]
    for cp in loads:
        cp.start()

    barrier = pltpu.get_barrier_semaphore()
    for peer in (succ, pred, sib, cross):
        pl.semaphore_signal(barrier, inc=1, device_id=peer, device_id_type=MESH)
    pl.semaphore_wait(barrier, 4)

    owns = [pltpu.make_async_copy(inputs[p], at(p, 0, q), own_sem.at[p]) for p in range(2)]
    for cp in owns:
        cp.start()

    def remote(p, src, k, col, peer, sem):
        return pltpu.make_async_remote_copy(
            src_ref=src,
            dst_ref=at(p, k, col),
            send_sem=sem.at[p],
            recv_sem=recv_sem.at[p, k, col],
            device_id=peer,
            device_id_type=MESH,
        )

    def source(p, k, col):
        return inputs[p] if k == 0 else at(p, k, col)

    sends = []
    for k in range(DEPTH):
        if k > 0:
            for p in range(2):
                remote(p, source(p, k, q), k, q, pred, relay_sem.at[k - 1]).wait_recv()
        if k + 1 < DEPTH:
            for p in range(2):
                cp = remote(p, source(p, k, q), k + 1, q, succ, relay_sem.at[k])
                cp.start()
                sends.append(cp)
        for p in range(2):
            cp = remote(p, source(p, k, q), k, q, cross, cross_sem.at[k])
            cp.start()
            sends.append(cp)
        for p in range(2):
            cp = remote(p, source(p, k, q), k, q, sib, sib_sem.at[k])
            cp.start()
            sends.append(cp)
        if k == 0:
            loads[0].wait()
            loads[1].wait()
            head = lax.broadcasted_iota(jnp.int32, (heads, BLK), 0)
            win8 = jnp.zeros((heads, BLK), jnp.int32)
            for h in range(heads):
                win8 = jnp.where(head == h, win_ref[h], win8)
            doc_here = docs_ref[g]
            for slot in range(DEPTH * LEVEL):
                d = LEVEL * (slot // LEVEL) + q - slot % LEVEL
                kb = g - d
                doc_there = docs_ref[(kb + n_blocks) % n_blocks]
                live = (d >= 0) & (d < WMAX) & (kb >= 0) & (doc_there == doc_here)
                keep = (win8 > d) & (jnp.full((heads, BLK), live.astype(jnp.int32)) > 0)
                bias_sc[:, pl.ds(slot * BLK, BLK)] = jnp.where(keep, 0.0, -jnp.inf).astype(jnp.float32)

    for k in range(DEPTH):
        for p in range(2):
            got_cross = at(p, k, cross_q)
            remote(p, got_cross, k, cross_q, cross, cross_sem.at[k]).wait_recv()
            cp = remote(p, got_cross, k, cross_q, sib, fwd_sem.at[k])
            cp.start()
            sends.append(cp)

    for k in range(DEPTH):
        for p in range(2):
            remote(p, at(p, k, sib_q), k, sib_q, sib, sib_sem.at[k]).wait_recv()
        for p in range(2):
            remote(p, at(p, k, far_q), k, far_q, sib, fwd_sem.at[k]).wait_recv()
    for cp in owns:
        cp.wait()
    loads[2].wait()

    scale = hd ** -0.5
    own = pl.multiple_of(q * BLK, BLK)

    def one_chunk(ci, carry):
        r0 = pl.multiple_of(ci * chunk, chunk)
        qc = q_ref[pl.ds(r0, chunk), :]
        sc = lax.dot_general(qc, got_k[...], (((1,), (1,)), ((), ())), preferred_element_type=jnp.float32) * scale
        sc = (sc.reshape(chunk // heads, heads, keys) + bias_sc[...][None]).reshape(chunk, keys)
        s_sc[...] = sc
        query_i = (lax.broadcasted_iota(jnp.int32, (chunk, BLK), 0) + r0) // heads
        key_j = lax.broadcasted_iota(jnp.int32, (chunk, BLK), 1)
        s_sc[:, pl.ds(own, BLK)] = jnp.where(key_j <= query_i, s_sc[:, pl.ds(own, BLK)], -jnp.inf)
        sc = s_sc[...]
        m = jnp.max(sc, axis=1, keepdims=True)
        w = jnp.exp(sc - m).astype(jnp.bfloat16)
        num = jnp.dot(w, got_v[...], preferred_element_type=jnp.float32)
        den = jnp.sum(w.astype(jnp.float32), axis=1, keepdims=True)
        out_ref[pl.ds(r0, chunk), :] = (num / den).astype(out_ref.dtype)
        return carry

    lax.fori_loop(0, rows // chunk, one_chunk, 0)

    for cp in sends:
        cp.wait_send()


def fused(block_docs, windows, key_rows, value_rows, q2, n_ctx, n_sub):
    rows, hd = q2.shape
    keys = DEPTH * LEVEL * BLK
    chunk = 1024
    heads = windows.shape[0]
    return pl.pallas_call(
        functools.partial(fused_kernel, n_ctx, n_sub),
        out_shape=jax.ShapeDtypeStruct((rows, hd), q2.dtype),
        in_specs=[pl.BlockSpec(memory_space=pltpu.HBM)] * 5,
        out_specs=pl.BlockSpec(memory_space=pltpu.VMEM),
        scratch_shapes=[
            pltpu.VMEM((keys, hd), key_rows.dtype),
            pltpu.VMEM((keys, hd), value_rows.dtype),
            pltpu.VMEM((heads, keys), jnp.float32),
            pltpu.VMEM((chunk, keys), jnp.float32),
            pltpu.VMEM((rows, hd), q2.dtype),
            pltpu.SMEM(block_docs.shape, jnp.int32),
            pltpu.SMEM(windows.shape, jnp.int32),
            pltpu.SemaphoreType.DMA((3,)),
            pltpu.SemaphoreType.DMA((2, DEPTH, LEVEL)),
            pltpu.SemaphoreType.DMA((DEPTH, 2)),
            pltpu.SemaphoreType.DMA((DEPTH, 2)),
            pltpu.SemaphoreType.DMA((DEPTH, 2)),
            pltpu.SemaphoreType.DMA((DEPTH, 2)),
            pltpu.SemaphoreType.DMA((2,)),
        ],
        compiler_params=pltpu.CompilerParams(
            collective_id=0, has_side_effects=True, vmem_limit_bytes=67043328
        ),
    )(block_docs, windows, key_rows, value_rows, q2)


def local(queries, key_rows, value_rows, block_docs, windows):
    n_ctx = lax.axis_size("ctx")
    n_sub = lax.axis_size("sub")
    rows_here, heads, hd = queries.shape
    out = fused(block_docs, windows, key_rows, value_rows, queries.reshape(rows_here * heads, hd), n_ctx, n_sub)
    return out.reshape(rows_here, heads, hd)


def solution(mesh):
    in_specs = (
        P(("ctx", "sub"), None, None),
        P(("ctx", "sub"), None),
        P(("ctx", "sub"), None),
        P(),
        P(),
    )
    out_specs = P(("ctx", "sub"), None, None)
    return jax.shard_map(local, mesh=mesh, in_specs=in_specs, out_specs=out_specs, check_vma=False)
```

```python
import functools

import jax
import jax.numpy as jnp
from jax import lax
from jax.experimental import pallas as pl
from jax.experimental.pallas import tpu as pltpu
from jax.sharding import PartitionSpec as P

BLK = 128
WMAX = 32
LEVEL = 4
DEPTH = (WMAX - 1 + LEVEL - 1) // LEVEL + 1
MESH = pl.DeviceIdType.MESH


def fused_kernel(n_ctx, n_sub, docs_hbm, win_hbm, k_ref, v_ref, q_hbm, out_ref,
                 got_k, got_v, bias_sc, s_sc, q_ref, docs_ref, win_ref, v_ones, in_sem,
                 recv_sem, relay_sem, sib_sem, cross_sem, fwd_sem, own_sem):
    c = lax.axis_index("ctx")
    s = lax.axis_index("sub")
    total = n_ctx * n_sub
    g = c * n_sub + s
    q = s % LEVEL
    succ_g = (g + LEVEL) % total
    pred_g = (g + total - LEVEL) % total
    succ = (succ_g // n_sub, succ_g % n_sub)
    pred = (pred_g // n_sub, pred_g % n_sub)
    sib_q = q + 1 - 2 * (q % 2)
    cross_q = q + 2 - 4 * ((q // 2) % 2)
    far_q = 3 - q
    sib = (c, s - q + sib_q)
    cross = (c, s - q + cross_q)
    planes = (got_k, got_v)
    inputs = (k_ref, v_ref)
    rows, hd = q_ref.shape
    chunk, keys = s_sc.shape
    heads = bias_sc.shape[0]
    n_blocks = docs_ref.shape[0]

    def at(p, k, col):
        return planes[p].at[pl.ds(pl.multiple_of((k * LEVEL + col) * BLK, BLK), BLK)]

    loads = [
        pltpu.make_async_copy(docs_hbm, docs_ref, in_sem.at[0]),
        pltpu.make_async_copy(win_hbm, win_ref, in_sem.at[1]),
        pltpu.make_async_copy(q_hbm, q_ref, in_sem.at[2]),
    ]
    for cp in loads:
        cp.start()

    barrier = pltpu.get_barrier_semaphore()
    for peer in (succ, pred, sib, cross):
        pl.semaphore_signal(barrier, inc=1, device_id=peer, device_id_type=MESH)
    pl.semaphore_wait(barrier, 4)

    owns = [pltpu.make_async_copy(inputs[p], at(p, 0, q), own_sem.at[p]) for p in range(2)]
    for cp in owns:
        cp.start()

    def remote(p, src, k, col, peer, sem):
        return pltpu.make_async_remote_copy(
            src_ref=src,
            dst_ref=at(p, k, col),
            send_sem=sem.at[p],
            recv_sem=recv_sem.at[p, k, col],
            device_id=peer,
            device_id_type=MESH,
        )

    def source(p, k, col):
        return inputs[p] if k == 0 else at(p, k, col)

    sends = []
    for k in range(DEPTH):
        if k > 0:
            for p in range(2):
                remote(p, source(p, k, q), k, q, pred, relay_sem.at[k - 1]).wait_recv()
        if k + 1 < DEPTH:
            for p in range(2):
                cp = remote(p, source(p, k, q), k + 1, q, succ, relay_sem.at[k])
                cp.start()
                sends.append(cp)
        for p in range(2):
            cp = remote(p, source(p, k, q), k, q, cross, cross_sem.at[k])
            cp.start()
            sends.append(cp)
        for p in range(2):
            cp = remote(p, source(p, k, q), k, q, sib, sib_sem.at[k])
            cp.start()
            sends.append(cp)
        if k == 0:
            loads[0].wait()
            loads[1].wait()
            head = lax.broadcasted_iota(jnp.int32, (heads, BLK), 0)
            win8 = jnp.zeros((heads, BLK), jnp.int32)
            for h in range(heads):
                win8 = jnp.where(head == h, win_ref[h], win8)
            doc_here = docs_ref[g]
            for slot in range(DEPTH * LEVEL):
                d = LEVEL * (slot // LEVEL) + q - slot % LEVEL
                kb = g - d
                doc_there = docs_ref[(kb + n_blocks) % n_blocks]
                live = (d >= 0) & (d < WMAX) & (kb >= 0) & (doc_there == doc_here)
                keep = (win8 > d) & (jnp.full((heads, BLK), live.astype(jnp.int32)) > 0)
                bias_sc[:, pl.ds(slot * BLK, BLK)] = jnp.where(keep, 0.0, -jnp.inf).astype(jnp.float32)

    for k in range(DEPTH):
        for p in range(2):
            got_cross = at(p, k, cross_q)
            remote(p, got_cross, k, cross_q, cross, cross_sem.at[k]).wait_recv()
            cp = remote(p, got_cross, k, cross_q, sib, fwd_sem.at[k])
            cp.start()
            sends.append(cp)

    for k in range(DEPTH):
        for p in range(2):
            remote(p, at(p, k, sib_q), k, sib_q, sib, sib_sem.at[k]).wait_recv()
        for p in range(2):
            remote(p, at(p, k, far_q), k, far_q, sib, fwd_sem.at[k]).wait_recv()
    for cp in owns:
        cp.wait()
    loads[2].wait()
    v_ones[:, :hd] = got_v[...]
    v_ones[:, hd:] = jnp.ones((keys, BLK), got_v.dtype)

    scale = hd ** -0.5
    own = pl.multiple_of(q * BLK, BLK)

    def one_chunk(ci, carry):
        r0 = pl.multiple_of(ci * chunk, chunk)
        qc = q_ref[pl.ds(r0, chunk), :]
        sc = lax.dot_general(qc, got_k[...], (((1,), (1,)), ((), ())), preferred_element_type=jnp.float32) * scale
        sc = (sc.reshape(chunk // heads, heads, keys) + bias_sc[...][None]).reshape(chunk, keys)
        s_sc[...] = sc
        query_i = (lax.broadcasted_iota(jnp.int32, (chunk, BLK), 0) + r0) // heads
        key_j = lax.broadcasted_iota(jnp.int32, (chunk, BLK), 1)
        s_sc[:, pl.ds(own, BLK)] = jnp.where(key_j <= query_i, s_sc[:, pl.ds(own, BLK)], -jnp.inf)
        sc = s_sc[...]
        m = jnp.max(sc, axis=1, keepdims=True)
        w = jnp.exp(sc - m).astype(jnp.bfloat16)
        both = jnp.dot(w, v_ones[...], preferred_element_type=jnp.float32)
        out_ref[pl.ds(r0, chunk), :] = (both[:, :hd] / both[:, hd:hd + 1]).astype(out_ref.dtype)
        return carry

    lax.fori_loop(0, rows // chunk, one_chunk, 0)

    for cp in sends:
        cp.wait_send()


def fused(block_docs, windows, key_rows, value_rows, q2, n_ctx, n_sub):
    rows, hd = q2.shape
    keys = DEPTH * LEVEL * BLK
    chunk = 1024
    heads = windows.shape[0]
    return pl.pallas_call(
        functools.partial(fused_kernel, n_ctx, n_sub),
        out_shape=jax.ShapeDtypeStruct((rows, hd), q2.dtype),
        in_specs=[pl.BlockSpec(memory_space=pltpu.HBM)] * 5,
        out_specs=pl.BlockSpec(memory_space=pltpu.VMEM),
        scratch_shapes=[
            pltpu.VMEM((keys, hd), key_rows.dtype),
            pltpu.VMEM((keys, hd), value_rows.dtype),
            pltpu.VMEM((heads, keys), jnp.float32),
            pltpu.VMEM((chunk, keys), jnp.float32),
            pltpu.VMEM((rows, hd), q2.dtype),
            pltpu.SMEM(block_docs.shape, jnp.int32),
            pltpu.SMEM(windows.shape, jnp.int32),
            pltpu.VMEM((keys, hd + BLK), value_rows.dtype),
            pltpu.SemaphoreType.DMA((3,)),
            pltpu.SemaphoreType.DMA((2, DEPTH, LEVEL)),
            pltpu.SemaphoreType.DMA((DEPTH, 2)),
            pltpu.SemaphoreType.DMA((DEPTH, 2)),
            pltpu.SemaphoreType.DMA((DEPTH, 2)),
            pltpu.SemaphoreType.DMA((DEPTH, 2)),
            pltpu.SemaphoreType.DMA((2,)),
        ],
        compiler_params=pltpu.CompilerParams(
            collective_id=0, has_side_effects=True, vmem_limit_bytes=67043328
        ),
    )(block_docs, windows, key_rows, value_rows, q2)


def local(queries, key_rows, value_rows, block_docs, windows):
    n_ctx = lax.axis_size("ctx")
    n_sub = lax.axis_size("sub")
    rows_here, heads, hd = queries.shape
    out = fused(block_docs, windows, key_rows, value_rows, queries.reshape(rows_here * heads, hd), n_ctx, n_sub)
    return out.reshape(rows_here, heads, hd)


def solution(mesh):
    in_specs = (
        P(("ctx", "sub"), None, None),
        P(("ctx", "sub"), None),
        P(("ctx", "sub"), None),
        P(),
        P(),
    )
    out_specs = P(("ctx", "sub"), None, None)
    return jax.shard_map(local, mesh=mesh, in_specs=in_specs, out_specs=out_specs, check_vma=False)
```
